32 devices in a mesh: seq: 4 (over x, core), exp: 2 (over y), ff: 4 (over z).
Axes of the slice: x: 2, y: 2, z: 4, core: 2. Of those that a mesh axis runs over, the one named last changes fastest.
Arguments:
- query_proj: bfloat16 [2, 512, 2560], P('exp', 'seq', 'ff'), may hold values from -85 to 85
- key_proj: bfloat16 [2, 512, 512], P('exp', 'seq', 'ff'), may hold values from -4.2 to 4.2
- value_proj: bfloat16 [2, 512, 512], P('exp', 'seq', 'ff'), may hold values from -6 to 6
- residual: bfloat16 [2, 512, 2560], P('exp', 'seq', 'ff'), may hold values from -60 to 60
- norm_gain: float32 [2560], P('ff'), may hold values from 0.5 to 2
- router_logit: float32 [2, 512], P('exp', 'seq'), may hold values from 1 to 6
- expert_ids: int32 [2, 512, 1], P('exp', 'seq'), may hold values from 0 to 1; in each aligned block of 128 rows (0 to 127, 128 to 255, ..., all dimensions but the last counted through in order) at most 96 rows name the same one
- gate_weight: bfloat16 [2, 2560, 4096], P('exp', None, ('seq', 'ff')), may hold values from -0.125 to 0.125
- up_weight: bfloat16 [2, 2560, 4096], P('exp', None, ('seq', 'ff')), may hold values from -0.125 to 0.125
- down_weight: bfloat16 [2, 4096, 2560], P('exp', ('seq', 'ff')), may hold values from -0.125 to 0.125
Outputs:
- layer_out: bfloat16 [2, 512, 2560], P('exp', 'seq', 'ff')
The draws below stay inside these ranges and needn't reach their ends.
Inputs may be any that keep to these rules, and one draw needn't show every extreme that they name: `expert_ids`: within each aligned block of 128 positions of a span (the positions of one index of seq), no expert is named by more than 96 tokens, and in some blocks an expert is named by exactly 96.
All inputs are finite; a program needn't handle non-finite values.
Results may differ from the reference program's by a relative error of at most 0.015.
Values may be sent and summed in bfloat16 or wider, within the bound.
No kernel may reach another device: no remote copies, remote signals or barrier semaphores. Data moves between devices by JAX's collectives and lax.ppermute only.
A program may use at most 64 MiB of HBM per device.

```python
import math
import jax
import jax.numpy as jnp
import numpy as np
from jax import lax

HD = 128
HEADS = 20
KVH = 4
D = 2560
FF = 4096
SHARD = 128
SPAN = 512
SPANS = 2
EXPERTS = 2
CAP = 96
N_SEQ = 4
N_FF = 4


def base_keys(key):
    rows = jnp.clip(jax.random.normal(jax.random.fold_in(key, 101), (SPANS, SPAN, KVH * HD), jnp.float32), -4.0, 4.0)
    return rows


def draw_key_proj(key, part):
    return base_keys(key).astype(jnp.bfloat16)


def draw_query_proj(key, part):
    rows = jnp.clip(jax.random.normal(jax.random.fold_in(key, 103), (SPANS, SPAN, HEADS * HD), jnp.float32), -4.0, 4.0)
    return rows.astype(jnp.bfloat16)


def draw_residual(key, part):
    base = jnp.clip(jax.random.normal(jax.random.fold_in(key, 105), (SPANS, SPAN, D), jnp.float32), -5.0, 5.0)
    row_scale = jnp.exp(jax.random.uniform(jax.random.fold_in(key, 106), (SPANS, SPAN, 1), jnp.float32, -1.15, 1.15))
    direction = jnp.where(jax.random.uniform(jax.random.fold_in(key, 107), (), jnp.float32) < 0.5, -1.0, 1.0)
    ramp = jnp.linspace(-1.0, 1.0, D)[None, None, :]
    jitter = jax.random.uniform(jax.random.fold_in(key, 108), (1, 1, D), jnp.float32, -0.4, 0.4)
    col_scale = jnp.exp(0.9 * direction * ramp + jitter)
    return (base * row_scale * col_scale).astype(jnp.bfloat16)


def strengthened(drawn, rng, source, target, shards_of, factor):
    def block_of(dim):
        return (jnp.arange(drawn.shape[dim]) // (drawn.shape[dim] // shards_of)).reshape((-1,) + (1,) * (drawn.ndim - 1 - dim))

    near = jax.random.permutation(rng, shards_of)[block_of(target)]
    far = (block_of(target) + shards_of // 2) % shards_of
    return jnp.where((block_of(source) == near) | (block_of(source) == far), factor * drawn, drawn)


def block_scale(stream_key, extent, cuts, least, high):
    def one(dim, blocks):
        steps = jax.random.uniform(jax.random.fold_in(jax.random.fold_in(stream_key, 6), dim), (blocks,), jnp.float32, least / len(cuts), high / len(cuts))
        return jnp.repeat(jnp.exp(steps), extent[dim] // blocks).reshape((-1,) + (1,) * (len(extent) - dim - 1))

    gain = one(*cuts[0])
    for cut in cuts[1:]:
        gain = gain * one(*cut)
    return gain


def deal_out(rng, own, number, rows, amount, top, most, skew):
    order = jax.random.permutation(rng, amount)
    heavy_load, ordinary = portions_of(amount, rows * top, most, skew, True), portions_of(amount, rows * top, most, skew, False)
    places = jnp.arange(amount)

    def named(sizes, turn):
        used = int((sizes > 0).sum())
        fixed = max(1, used // 4)
        shifted = fixed + (places - fixed + turn * (used - fixed)) % max(1, amount - fixed)
        return jnp.zeros((amount,), jnp.int32).at[order[jnp.where(places < fixed, places, shifted)]].set(jnp.asarray(sizes, jnp.int32))

    sizes = jnp.where(number % 4 == 0, named(heavy_load, number // 4), named(ordinary, number - number // 4 - 1))
    mixed = jax.random.permutation(jax.random.fold_in(own, 3), amount)
    giver, receiver = mixed[0:amount // 2 * 2:2], mixed[1:amount // 2 * 2:2]
    room = jnp.minimum(sizes[giver] - 1, most - sizes[receiver]) // 2
    room = jnp.where((giver == order[0]) | (receiver == order[0]) | (sizes[receiver] == 0), 0, jnp.maximum(room, 0))
    shifted = jax.random.randint(jax.random.fold_in(own, 4), (amount // 2,), 0, 1 << 20) % (room + 1)
    sizes = sizes.at[giver].add(-shifted).at[receiver].add(shifted)
    labels = jnp.searchsorted(jnp.cumsum(sizes), jnp.arange(rows * top), side="right").astype(jnp.int32)
    table = labels.reshape(top, rows).T
    table = table[jax.random.permutation(jax.random.fold_in(own, 1), rows)]
    turn = jax.random.randint(jax.random.fold_in(own, 2), (rows, 1), 0, top)
    return jnp.take_along_axis(table, (jnp.arange(top)[None, :] + turn) % top, axis=1)


def portions_of(count, total, bound, skew, full):
    portions = [(1 << 20) // math.isqrt(standing ** skew) + 1 for standing in range(1, count + 1)]
    largest = bound if full else min(bound, max(-(-total // count), total * portions[0] // sum(portions)))
    least = 1 if total - largest >= count - 1 else 0
    given, surplus = [largest] + [least] * (count - 1), total - largest - least * (count - 1)
    while surplus > 0:
        candidates = [i for i in range(1, count) if given[i] < largest] or [i for i in range(1, count) if given[i] < bound]
        pool, budget = sum([portions[i] for i in candidates]), surplus
        for i in candidates:
            extra = min(bound - given[i], max(1, budget * portions[i] // pool), surplus)
            given[i] = given[i] + extra
            surplus = surplus - extra
    return np.array(given)


def scatter_about(key, dims, spread, bound, shards=(), kind=jnp.bfloat16):
    array = spread * jax.random.normal(key, dims, jnp.float32)
    if shards:
        array = array * block_scale(key, dims, shards, -0.22, 0.18)
    return jnp.clip(array, -bound, bound).astype(kind)


def gaussian_with(stream_key, dims, width, most, cuts, heavy, kind=jnp.bfloat16):
    values = width * jax.random.normal(stream_key, dims, jnp.float32)
    if cuts:
        values = values * block_scale(stream_key, dims, cuts, -0.22, 0.18)
    return jnp.clip(strengthened(values, jax.random.fold_in(stream_key, 3), *heavy), -most, most).astype(kind)


def setup_inputs(seed: int = 0) -> dict:
    seeds = jax.random.split(jax.random.key(seed), 11)
    query_proj = draw_query_proj(jax.random.fold_in(seeds[10], 71), 0)
    key_proj = draw_key_proj(jax.random.fold_in(seeds[10], 71), 0)
    value_proj = scatter_about(seeds[2], (SPANS, SPAN, KVH * HD), 1.0, 6.0, ((0, 2), (1, 4), (2, 4)))
    residual = draw_residual(jax.random.fold_in(seeds[10], 71), 0)
    norm_gain = jnp.clip(jnp.exp(math.log(2.0) - 1.3862944 * jax.random.uniform(seeds[4], (D,), jnp.float32) ** block_scale(seeds[4], (D,), ((0, 4),), -0.2, 0.2)), 0.5, 2.0)
    router_logit = jnp.clip(1.0 + 5.0 * jax.random.uniform(seeds[5], (SPANS, SPAN), jnp.float32) ** block_scale(seeds[5], (SPANS, SPAN), ((0, 2), (1, 4)), -0.2, 0.2), 1.0, 6.0)
    expert_ids_keys = jax.random.split(jax.random.fold_in(seeds[6], 1), SPANS * SPAN // SHARD)
    expert_ids_turns = jax.random.permutation(jax.random.fold_in(seeds[6], 3), SPANS * SPAN // SHARD)
    expert_ids = jax.vmap(lambda own, number: deal_out(jax.random.fold_in(seeds[6], 2), own, number, SHARD, EXPERTS, 1, CAP, 2))(expert_ids_keys, expert_ids_turns).reshape((SPANS, SPAN, 1))
    gate_weight = scatter_about(seeds[7], (EXPERTS, D, FF), D ** -0.5, 0.125, ((0, 2), (2, 16)))
    up_weight = scatter_about(seeds[8], (EXPERTS, D, FF), D ** -0.5, 0.125, ((0, 2), (2, 16)))
    down_weight = gaussian_with(seeds[9], (EXPERTS, FF, D), FF ** -0.5, 0.125, ((0, 2), (1, 16)), (1, 2, 16, 2.0))
    return {"query_proj": query_proj, "key_proj": key_proj, "value_proj": value_proj, "residual": residual, "norm_gain": norm_gain, "router_logit": router_logit, "expert_ids": expert_ids, "gate_weight": gate_weight, "up_weight": up_weight, "down_weight": down_weight}


floor_score = -1e+30
norm_eps = 1e-05

def span_attention(pieces):
    queries, keys_in, values_in = pieces
    group = HEADS // KVH
    query_f = queries.astype(jnp.float32).reshape(SPAN, KVH, group, HD)
    key_f = keys_in.astype(jnp.float32).reshape(SPAN, KVH, HD)
    value_f = values_in.astype(jnp.float32).reshape(SPAN, KVH, HD)
    scores = jnp.einsum('qagd,kad->agqk', query_f, key_f, precision=lax.Precision.HIGHEST) * HD ** (-0.5)
    positions = lax.iota(jnp.int32, SPAN)
    allowed = positions[None, :] <= positions[:, None]
    masked = jnp.where(allowed, scores, floor_score)
    peak = lax.optimization_barrier(jnp.max(masked, axis=-1))
    weights = jnp.where(allowed, jnp.exp(masked - peak[..., None]), 0.0)
    rounded = lax.optimization_barrier(weights.astype(jnp.bfloat16)).astype(jnp.float32)
    mixed = jnp.einsum('agqk,kad->agqd', rounded, value_f, precision=lax.Precision.HIGHEST)
    mixed = mixed / lax.optimization_barrier(jnp.sum(weights, axis=-1))[..., None]
    return mixed.transpose(2, 0, 1, 3).reshape(SPAN, HEADS * HD)

def reference(query_proj, key_proj, value_proj, residual, norm_gain, router_logit, expert_ids, gate_weight, up_weight, down_weight):
    attention = lax.map(span_attention, (query_proj, key_proj, value_proj))
    stream = (residual.astype(jnp.float32) + attention).astype(jnp.bfloat16)
    stream_f = stream.astype(jnp.float32)
    meansq = lax.optimization_barrier(jnp.mean(stream_f * stream_f, axis=-1))
    routed_in = stream_f * lax.rsqrt(meansq + norm_eps)[..., None] * norm_gain * jax.nn.sigmoid(router_logit)[..., None]
    routed_in = routed_in.astype(jnp.bfloat16)
    route = expert_ids[..., 0]
    onehot = (route[..., None] == jnp.arange(EXPERTS, dtype=jnp.int32)).astype(jnp.float32)
    blocks = onehot.reshape(SPANS, N_SEQ, SHARD, EXPERTS)
    earlier = jnp.cumsum(blocks, axis=2) - blocks
    slot = lax.optimization_barrier(jnp.sum(earlier * blocks, axis=-1)).astype(jnp.int32)
    span_index = jnp.arange(SPANS, dtype=jnp.int32)[:, None, None]
    shard_index = jnp.arange(N_SEQ, dtype=jnp.int32)[None, :, None]
    position = ((shard_index * EXPERTS + span_index) * CAP + slot).reshape(-1)
    route_flat = route.reshape(-1)
    routed_flat = routed_in.reshape(-1, D)
    rows_all = N_SEQ * EXPERTS * CAP
    groups = N_SEQ * N_FF
    unit_count = FF // groups

    def expert_output(expert):
        slot_index = jnp.where(route_flat == expert, position, rows_all)
        buffer = jnp.zeros((rows_all, D), jnp.bfloat16).at[slot_index].set(routed_flat, mode='drop')
        gate = jnp.dot(buffer, gate_weight[expert], preferred_element_type=jnp.float32)
        upward = jnp.dot(buffer, up_weight[expert], preferred_element_type=jnp.float32)
        activated = (jax.nn.silu(gate) * upward).astype(jnp.bfloat16)
        parts = jnp.einsum('rgk,gkd->grd', activated.astype(jnp.float32).reshape(rows_all, groups, unit_count), down_weight[expert].astype(jnp.float32).reshape(groups, unit_count, D), precision=lax.Precision.HIGHEST)
        parts = lax.optimization_barrier(parts.astype(jnp.bfloat16)).astype(jnp.float32)
        return lax.optimization_barrier(jnp.sum(parts, axis=0)).astype(jnp.bfloat16)
    expert_all = lax.map(expert_output, jnp.arange(EXPERTS, dtype=jnp.int32))
    picked = expert_all[route_flat, position]
    layer_out = stream_f.reshape(-1, D) + picked.astype(jnp.float32)
    return layer_out.astype(jnp.bfloat16).reshape(SPANS, SPAN, D)
```

```python
import functools
import jax
import jax.numpy as jnp
from jax import lax
from jax.experimental import pallas as pl
from jax.experimental.pallas import tpu as pltpu
from jax.sharding import PartitionSpec as P

HD = 128
HEADS = 20
KVH = 4
D = 2560

floor_score = -1e30
norm_eps = 1e-05
f32 = jnp.float32
bf16 = jnp.bfloat16


def ring(value, axis, step):
    n = lax.axis_size(axis)
    return lax.ppermute(value, axis, [(i, (i + step) % n) for i in range(n)])


def flip(value, axis, bit):
    n = lax.axis_size(axis)
    return lax.ppermute(value, axis, [(i, i ^ bit) for i in range(n)])


def to_later(value, axis, bit):
    n = lax.axis_size(axis)
    return lax.ppermute(value, axis, [(i, i ^ bit) for i in range(n) if i < i ^ bit])


def attend(group, blocks, *refs):
    where_ref, q_ref, res_ref, target_ref = refs[:4]
    k_refs = refs[4 : 4 + blocks]
    v_refs = refs[4 + blocks : 4 + 2 * blocks]
    stream_ref, send_ref = refs[4 + 2 * blocks :]
    shard = q_ref.shape[0]
    me = where_ref[0]
    rows = lax.broadcasted_iota(jnp.int32, (shard, shard), 0)
    cols = lax.broadcasted_iota(jnp.int32, (shard, shard), 1)
    nt = (((1,), (1,)), ((), ()))
    pieces = []
    for h in range(q_ref.shape[1] // HD):
        g = h // group
        q = q_ref[:, h * HD : (h + 1) * HD]
        scores = []
        for b in range(blocks):
            s = lax.dot_general(q, k_refs[b][:, g * HD : (g + 1) * HD], nt, preferred_element_type=f32)
            s = s * HD ** (-0.5)
            ok = cols <= rows if b == 0 else cols < jnp.where((me ^ b) < me, shard, 0)
            scores.append(jnp.where(ok, s, floor_score))
        top = functools.reduce(jnp.maximum, scores)
        top = jnp.max(top, axis=1, keepdims=True)
        total = jnp.zeros((shard, 1), f32)
        acc = jnp.zeros((shard, HD), f32)
        weights = [jnp.exp(s - top) for s in scores]
        total = jnp.sum(functools.reduce(jnp.add, weights), axis=1, keepdims=True)
        for b in range(blocks):
            acc += jnp.dot(weights[b].astype(bf16), v_refs[b][:, g * HD : (g + 1) * HD], preferred_element_type=f32)
        pieces.append(acc / total)
    stream = (res_ref[...].astype(f32) + jnp.concatenate(pieces, axis=1)).astype(bf16)
    stream_ref[...] = stream
    slots = send_ref.shape[0]
    pick = (lax.broadcasted_iota(jnp.int32, (slots, shard), 0) == target_ref[...]).astype(bf16)
    send_ref[...] = jnp.dot(pick, stream, preferred_element_type=f32).astype(bf16)


def attention(me, query, residual, target_row, keys, values, slots):
    shard, width = query.shape
    group = HEADS // KVH
    blocks = len(keys)
    return pl.pallas_call(
        functools.partial(attend, group, blocks),
        out_shape=(
            jax.ShapeDtypeStruct((shard, width), bf16),
            jax.ShapeDtypeStruct((slots, width), bf16),
        ),
        in_specs=[pl.BlockSpec(memory_space=pltpu.SMEM)]
        + [pl.BlockSpec(memory_space=pltpu.VMEM)] * (3 + 2 * blocks),
        out_specs=(pl.BlockSpec(memory_space=pltpu.VMEM),) * 2,
        compiler_params=pltpu.CompilerParams(vmem_limit_bytes=16 << 20),
        name="attend",
    )(me, query, residual, target_row, *keys, *values)


def mlp_body(where_ref, scale_ref, gain_ref, *refs):
    count = gain_ref.shape[0]
    x_refs = refs[:count]
    gates, ups, downs = refs[count : count + 2], refs[count + 2 : count + 4], refs[count + 4 : count + 6]
    out_refs = refs[count + 6 :]
    rows, quarter = x_refs[0].shape
    mine = where_ref[0]
    squares = jnp.zeros((rows, 1), f32)
    hidden = gates[0].shape[1]
    g = [jnp.zeros((rows, hidden), f32) for _ in gates]
    u = [jnp.zeros((rows, hidden), f32) for _ in ups]
    for i, x_ref in enumerate(x_refs):
        at = lax.rem(mine + i, count)
        wide = x_ref[...].astype(f32)
        squares += jnp.sum(wide * wide, axis=1, keepdims=True)
        x = (wide * gain_ref[i : i + 1, :]).astype(bf16)
        part = pl.ds(pl.multiple_of(at * quarter, quarter), quarter)
        for k in range(2):
            g[k] += jnp.dot(x, gates[k][part, :], preferred_element_type=f32)
            u[k] += jnp.dot(x, ups[k][part, :], preferred_element_type=f32)
    eye = lax.broadcasted_iota(jnp.int32, (rows, rows), 0) == lax.broadcasted_iota(jnp.int32, (rows, rows), 1)
    gated = jnp.sum(jnp.where(eye, scale_ref[...], 0.0), axis=1, keepdims=True)
    factor = lax.rsqrt(squares / (count * quarter) + norm_eps) * gated
    act = []
    for k in range(2):
        gate, up = g[k] * factor, u[k] * factor
        act.append((gate / (1.0 + jnp.exp(-gate)) * up).astype(bf16))
    for i, out_ref in enumerate(out_refs):
        at = lax.rem(mine + i, count)
        part = pl.ds(pl.multiple_of(at * quarter, quarter), quarter)
        y = jnp.dot(act[0], downs[0][:, part], preferred_element_type=f32)
        y += jnp.dot(act[1], downs[1][:, part], preferred_element_type=f32)
        out_ref[...] = y.astype(bf16)


def mlp(mine, scale, gains, blocks, weights):
    rows, quarter = blocks[0].shape
    return pl.pallas_call(
        mlp_body,
        out_shape=(jax.ShapeDtypeStruct((rows, quarter), bf16),) * len(blocks),
        in_specs=[pl.BlockSpec(memory_space=pltpu.SMEM)]
        + [pl.BlockSpec(memory_space=pltpu.VMEM)] * (2 + len(blocks) + len(weights)),
        out_specs=(pl.BlockSpec(memory_space=pltpu.VMEM),) * len(blocks),
        compiler_params=pltpu.CompilerParams(vmem_limit_bytes=32 << 20),
        name="mlp",
    )(mine, scale, gains, *blocks, *weights)


def add(*parts):
    total = parts[0].astype(f32)
    for part in parts[1:]:
        total = total + part.astype(f32)
    return total.astype(bf16)


def exchange(value):
    experts = lax.axis_size("exp")
    if experts == 2:
        half = value.shape[0] // 2
        return jnp.concatenate([value[:half], flip(value[half:], "exp", 1)], axis=0)
    return lax.all_to_all(value, "exp", split_axis=0, concat_axis=0, tiled=True)


def body(
    query_proj,
    key_proj,
    value_proj,
    residual,
    norm_gain,
    router_logit,
    expert_ids,
    gate_weight,
    up_weight,
    down_weight,
):
    shard = query_proj.shape[1]
    seq, experts, ff = lax.axis_size("seq"), lax.axis_size("exp"), lax.axis_size("ff")
    sid = lax.axis_index("seq").astype(jnp.int32)
    eid = lax.axis_index("exp").astype(jnp.int32)
    fid = lax.axis_index("ff").astype(jnp.int32)
    cap = max(2, 3 * shard // (2 * experts))
    slots = experts * cap
    quarter = query_proj.shape[2]

    keys, values = [key_proj[0]], [value_proj[0]]
    stacked = jnp.concatenate([key_proj[0], value_proj[0]], axis=0)
    for b in range(1, seq):
        got = to_later(stacked, "seq", b)
        keys.append(got[:shard])
        values.append(got[shard:])

    route = expert_ids[0, :, 0]
    if experts == 2:
        route = route ^ eid
    onehot = (route[:, None] == lax.iota(jnp.int32, experts)[None, :]).astype(bf16)
    row = lax.iota(jnp.int32, shard)
    below = (row[:, None] > row[None, :]).astype(bf16)
    earlier = jnp.dot(below, onehot, preferred_element_type=f32)
    slot = jnp.sum(earlier * onehot.astype(f32), axis=1).astype(jnp.int32)
    target = route * cap + slot
    taken = target[:, None] == lax.iota(jnp.int32, slots)[None, :]
    opened = jax.nn.sigmoid(router_logit[0])
    opened = jnp.sum(jnp.where(taken, opened[:, None], 0.0), axis=0)

    stream, outgoing = attention(sid[None], query_proj[0], residual[0], target[None, :], keys, values, slots)

    weights = (gate_weight[0], up_weight[0], down_weight[0])
    tied, small, outgoing_t = lax.optimization_barrier((weights, (norm_gain, opened), outgoing))
    block = exchange(outgoing)
    gains = jnp.stack([small[0]] + [ring(small[0], "ff", -i) for i in range(1, ff)])
    lit = exchange(small[1])
    lit_x = flip(lit, "seq", 2)
    partner = [flip(w, "seq", 1) for w in tied]
    pairs = [w for own in zip(weights, partner) for w in own]

    even = lax.rem(fid, 2) == 0
    x0 = flip(block, "seq", 2)
    low = ring(block, "ff", 1)
    high = ring(block, "ff", -1)
    sel = jnp.where(even, low, high)
    non = jnp.where(even, high, low)
    far = flip(sel, "ff", 1)
    sel_x = flip(sel, "seq", 2)
    non_x = flip(non, "seq", 2)
    far_x = flip(sel_x, "ff", 1)
    low_x = jnp.where(even, sel_x, non_x)
    high_x = jnp.where(even, non_x, sel_x)

    p0, p1, p2, p3 = mlp(fid[None], lit[None, :], gains, [block, high, far, low], pairs)
    o0, o1, o2, o3 = mlp(fid[None], lit_x[None, :], gains, [x0, high_x, far_x, low_x], pairs)

    psel, pnon = jnp.where(even, p3, p1), jnp.where(even, p1, p3)
    osel, onon = jnp.where(even, o3, o1), jnp.where(even, o1, o3)
    back_far_x = flip(o2, "ff", 1)
    back_far = flip(p2, "ff", 1)
    back0 = flip(o0, "seq", 2)
    back_non = flip(onon, "seq", 2)
    back_sel = flip(add(osel, back_far_x), "seq", 2)
    tot0 = p0.astype(f32) + back0.astype(f32)
    tot_non = add(pnon, back_non)
    tot_sel = add(psel, back_far, back_sel)
    to_low = jnp.where(even, tot_sel, tot_non)
    to_high = jnp.where(even, tot_non, tot_sel)
    summed = (tot0 + ring(to_low, "ff", -1).astype(f32) + ring(to_high, "ff", 1).astype(f32)).astype(bf16)
    returned = exchange(summed)
    combined = jnp.dot(taken.astype(bf16), returned, preferred_element_type=f32)
    return (stream.astype(f32) + combined).astype(bf16)[None]


def solution(mesh):
    placed = (
        P("exp", "seq", "ff"),
        P("exp", "seq", "ff"),
        P("exp", "seq", "ff"),
        P("exp", "seq", "ff"),
        P("ff"),
        P("exp", "seq"),
        P("exp", "seq", None),
        P("exp", None, ("seq", "ff")),
        P("exp", None, ("seq", "ff")),
        P("exp", ("seq", "ff"), None),
    )
    return jax.shard_map(
        body, mesh=mesh, in_specs=placed, out_specs=P("exp", "seq", "ff"), check_vma=False
    )
```

```python
import functools
import jax
import jax.numpy as jnp
from jax import lax
from jax.experimental import pallas as pl
from jax.experimental.pallas import tpu as pltpu
from jax.sharding import PartitionSpec as P

HD = 128
HEADS = 20
KVH = 4

floor_score = -1e30
norm_eps = 1e-05
EXTRA = 16
f32 = jnp.float32
bf16 = jnp.bfloat16
VMEM = pl.BlockSpec(memory_space=pltpu.VMEM)
SMEM = pl.BlockSpec(memory_space=pltpu.SMEM)
RAW = pl.BlockSpec(memory_space=pltpu.HBM)


def kernel(body, out, ins, outs, limit, scratch=(), cost=None):
    return pl.pallas_call(
        body,
        out_shape=out,
        in_specs=ins,
        out_specs=outs,
        scratch_shapes=scratch,
        compiler_params=pltpu.CompilerParams(vmem_limit_bytes=limit << 20),
        cost_estimate=cost,
    )


def flip(value, later=False, **bits):
    axes = tuple(bits)
    pairs = [((), ())]
    for axis in axes:
        n = lax.axis_size(axis)
        pairs = [(s + (i,), t + (i ^ bits[axis],)) for s, t in pairs for i in range(n)]

    def flat(index):
        total = 0
        for axis, i in zip(axes, index):
            total = total * lax.axis_size(axis) + i
        return total

    pairs = [(flat(s), flat(t)) for s, t in pairs]
    if later:
        pairs = [(s, t) for s, t in pairs if s < t]
    return lax.ppermute(value, axes, pairs)


def as_column(row):
    n = row.shape[1]
    eye = lax.broadcasted_iota(jnp.int32, (n, n), 0) == lax.broadcasted_iota(jnp.int32, (n, n), 1)
    return jnp.sum(jnp.where(eye, row, 0.0), axis=1, keepdims=True)


def pack_body(k_ref, v_ref, out_ref, sems):
    shard = k_ref.shape[1]
    copies = [
        pltpu.make_async_copy(k_ref.at[0], out_ref.at[pl.ds(0, shard)], sems.at[0]),
        pltpu.make_async_copy(v_ref.at[0], out_ref.at[pl.ds(shard, shard)], sems.at[1]),
    ]
    for c in copies:
        c.start()
    for c in copies:
        c.wait()


def split(value):
    high = value.astype(bf16)
    rest = value - high.astype(f32)
    middle = rest.astype(bf16)
    return [high, middle, (rest - middle.astype(f32)).astype(bf16)]


def prep_body(experts, cap, where_ref, q_in, res_in, ids_in, logit_in, gain_in, q_out, res_out, taken_ref, *refs):
    extra_refs = refs[: 2 if experts == 2 else 1]
    lit_ref, ids_ref, logit_ref, gain_ref, sems = refs[len(extra_refs) :]
    pairs = [(ids_in, ids_ref), (logit_in, logit_ref), (gain_in, gain_ref), (q_in.at[0], q_out), (res_in.at[0], res_out)]
    copies = [pltpu.make_async_copy(x, y, sems.at[i]) for i, (x, y) in enumerate(pairs)]
    for c in copies:
        c.start()
    copies[0].wait()
    shard = ids_ref.shape[1]
    slots = taken_ref.shape[1]
    route = as_column(ids_ref[...].astype(f32)).astype(jnp.int32)
    if experts == 2:
        route = route ^ where_ref[0]
    lanes = lax.broadcasted_iota(jnp.int32, (shard, shard), 1)
    rows = lax.broadcasted_iota(jnp.int32, (shard, shard), 0)
    onehot = (lanes == route).astype(f32)
    below = (rows > lanes).astype(bf16)
    earlier = jnp.dot(below, onehot.astype(bf16), preferred_element_type=f32)
    slot = jnp.sum(earlier * onehot, axis=1, keepdims=True).astype(jnp.int32)
    target = route * cap + slot
    taken = lax.broadcasted_iota(jnp.int32, (shard, slots), 1) == target
    taken_ref[...] = taken.astype(bf16)
    copies[1].wait()
    opened = as_column(1.0 / (1.0 + jnp.exp(-logit_ref[...])))
    lit = jnp.sum(jnp.where(taken, opened, 0.0), axis=0, keepdims=True)
    lit_ref[...] = lit
    copies[2].wait()
    width = gain_ref.shape[0]
    gain = gain_ref[...].reshape(1, width)
    none = [jnp.zeros((1, width), bf16)] * 3
    if experts == 2:
        full = [split(jnp.concatenate([part, jnp.zeros((1, width - cap), f32)], axis=1)) for part in (lit[:, :cap], lit[:, cap:])]
    else:
        full = [none]
    for ref, part, top in zip(extra_refs, full, (split(gain), none)):
        ref[...] = jnp.concatenate([*top, *part, jnp.zeros((EXTRA - 6, width), bf16)], axis=0)
    for c in copies[3:]:
        c.wait()


def attend_body(group, blocks, extras, layout, where_ref, q_ref, res_ref, taken_ref, *refs):
    kv_refs = refs[:blocks]
    extra_refs = refs[blocks : blocks + extras]
    stream_ref = refs[blocks + extras]
    send_refs = refs[blocks + extras + 1 :]
    shard = q_ref.shape[0]
    me = where_ref[0]
    rows = lax.broadcasted_iota(jnp.int32, (shard, shard), 0)
    cols = lax.broadcasted_iota(jnp.int32, (shard, shard), 1)
    nt = (((1,), (1,)), ((), ()))
    pieces = []
    for h in range(q_ref.shape[1] // HD):
        g = h // group
        q = q_ref[:, h * HD : (h + 1) * HD]
        scores = []
        for b in range(blocks):
            s = lax.dot_general(q, kv_refs[b][:shard, g * HD : (g + 1) * HD], nt, preferred_element_type=f32)
            s = s * HD ** (-0.5)
            ok = cols <= rows if b == 0 else cols < jnp.where((me ^ b) < me, shard, 0)
            scores.append(jnp.where(ok, s, floor_score))
        top = jnp.max(functools.reduce(jnp.maximum, scores), axis=1, keepdims=True)
        weights = [jnp.exp(s - top) for s in scores]
        total = jnp.sum(functools.reduce(jnp.add, weights), axis=1, keepdims=True)
        acc = jnp.zeros((shard, HD), f32)
        for b in range(blocks):
            acc += jnp.dot(weights[b].astype(bf16), kv_refs[b][shard:, g * HD : (g + 1) * HD], preferred_element_type=f32)
        pieces.append(acc / total)
    stream = (res_ref[...].astype(f32) + jnp.concatenate(pieces, axis=1)).astype(bf16)
    stream_ref[...] = stream
    tn = (((0,), (0,)), ((), ()))
    send = lax.dot_general(taken_ref[...], stream, tn, preferred_element_type=f32).astype(bf16)
    for ref, (at, rows, extra) in zip(send_refs, layout):
        ref[:rows] = send[at : at + rows]
        if extra is not None:
            ref[rows:] = extra_refs[extra][...]


def joined(refs, spans):
    parts = [refs[i][at : at + rows] for i, at, rows in spans]
    return parts[0] if len(parts) == 1 else jnp.concatenate(parts, axis=0)


def whole(ref, row, width):
    return sum(ref[row + i : row + i + 1, :width].astype(f32) for i in range(3))


def load_body(*refs):
    n = len(refs) // 2
    sems = refs[-1]
    copies = [pltpu.make_async_copy(refs[i], refs[n + i], sems.at[i]) for i in range(n)]
    for c in copies:
        c.start()
    for c in copies:
        c.wait()


def load(arrays):
    n = len(arrays)
    return kernel(
        load_body, [pltpu.VMEM(a.shape, a.dtype) for a in arrays], [RAW] * n, [VMEM] * n, 4,
        scratch=[pltpu.SemaphoreType.DMA((n,))],
    )(*[pltpu.with_memory_space_constraint(a, pltpu.HBM) for a in arrays])


def join_body(first_ref, second_ref, out_ref):
    rows = first_ref.shape[0]
    out_ref[:rows] = first_ref[...]
    out_ref[rows:] = second_ref[...]


def join(first, second):
    rows = first.shape[0] + second.shape[0]
    return kernel(join_body, pltpu.VMEM((rows, first.shape[1]), first.dtype), [VMEM] * 2, VMEM, 4)(first, second)


def mlp_body(spec, lit_of, cut, begun, where_ref, *refs):
    refs = list(refs)
    acc_in = [refs.pop(0) for _ in range(3)] if begun else None
    blocks = [([refs.pop(0) for _ in range(n)], spans, gain, i) for n, spans, gain, i in spec]
    lits = [refs.pop(0) for _ in lit_of]
    gates, ups = ([refs.pop(0) for _ in range(2)] for _ in range(2))
    mine = where_ref[0]
    g, u, squares = ([None, None], [None, None], None)
    if begun:
        hidden = gates[0].shape[1]
        g = [acc_in[0][:, k * hidden : (k + 1) * hidden] for k in range(2)]
        u = [acc_in[1][:, k * hidden : (k + 1) * hidden] for k in range(2)]
        squares = acc_in[2][:, :1]

    def plus(x, y):
        return y if x is None else x + y

    for arrays, spans, gain_row, i in blocks:
        at = mine ^ i
        wide = joined(arrays, spans).astype(f32)
        quarter = wide.shape[1]
        squares = plus(squares, jnp.sum(wide * wide, axis=1, keepdims=True))
        x = (wide * whole(arrays[0], gain_row, quarter)).astype(bf16)
        part = pl.ds(pl.multiple_of(at * quarter, quarter), quarter)
        for k in range(2):
            g[k] = plus(g[k], jnp.dot(x, gates[k][part, :], preferred_element_type=f32))
            u[k] = plus(u[k], jnp.dot(x, ups[k][part, :], preferred_element_type=f32))
    if not lit_of:
        g_ref, u_ref, s_ref = refs
        g_ref[...] = jnp.concatenate(g, axis=1)
        u_ref[...] = jnp.concatenate(u, axis=1)
        s_ref[...] = jnp.broadcast_to(squares, s_ref.shape)
        return
    downs = [refs.pop(0) for _ in range(2)]
    outs = [[refs.pop(0) for _ in range(n)] for n in (cut, 1, 1, 1)]
    quarter = outs[1][0].shape[1]
    opened = [as_column(whole(ref, row, n)) for ref, (row, n) in zip(lits, lit_of)]
    opened = opened[0] if len(opened) == 1 else jnp.concatenate(opened, axis=0)
    factor = lax.rsqrt(squares / (len(outs) * quarter) + norm_eps) * opened
    act = []
    for k in range(2):
        gate, up = g[k] * factor, u[k] * factor
        act.append((gate / (1.0 + jnp.exp(-gate)) * up).astype(bf16))
    for i in (2, 1, 3, 0):
        at = mine ^ i
        part = pl.ds(pl.multiple_of(at * quarter, quarter), quarter)
        y = jnp.dot(act[0], downs[0][:, part], preferred_element_type=f32)
        y += jnp.dot(act[1], downs[1][:, part], preferred_element_type=f32)
        y = y.astype(bf16)
        top = 0
        for ref in outs[i]:
            ref[...] = y[top : top + ref.shape[0]]
            top += ref.shape[0]


def mlp(mine, blocks, weights, cut=1, begun=None, lits=()):
    spec = [(len(arrays), spans, gain, i) for arrays, spans, gain, i in blocks]
    rows, quarter = sum(n for _, _, n in blocks[0][1]), blocks[0][0][0].shape[1]
    flat = [*(begun or ()), *[a for arrays, *_ in blocks for a in arrays], *[a for a, _, _ in lits]]
    hidden = weights[0].shape[1]
    flops = 2 * rows * quarter * len(blocks) * hidden * 4
    if lits:
        out = [pltpu.VMEM((rows // cut, quarter), bf16)] * cut + [pltpu.VMEM((rows, quarter), bf16)] * 3
        flops += 2 * rows * quarter * 4 * hidden * 2
    else:
        out = [pltpu.VMEM((rows, 2 * hidden), f32)] * 2 + [pltpu.VMEM((rows, HD), f32)]
        weights = weights[:4]
    weights = [pltpu.with_memory_space_constraint(w, pltpu.VMEM) for w in weights]
    out = kernel(
        functools.partial(mlp_body, spec, [(row, n) for _, row, n in lits], cut, begun is not None),
        out,
        [SMEM] + [VMEM] * (len(flat) + len(weights)),
        [VMEM] * len(out),
        12,
        cost=pl.CostEstimate(flops=flops, bytes_accessed=8 << 20, transcendentals=0),
    )(mine, *flat, *weights)
    return (out[:cut], *out[cut:]) if lits else out


def add(*parts):
    total = parts[0].astype(f32)
    for part in parts[1:]:
        total = total + part.astype(f32)
    return total.astype(bf16)


def final_body(shape, stream_ref, taken_ref, *refs):
    refs = list(refs)
    out_ref = refs.pop()
    total = stream_ref[...].astype(f32)
    at = 0
    for n in shape:
        part = refs.pop(0)[...].astype(f32)
        for _ in range(n - 1):
            part += refs.pop(0)[...].astype(f32)
        rows = part.shape[0]
        total += jnp.dot(taken_ref[:, at : at + rows], part.astype(bf16), preferred_element_type=f32)
        at += rows
    out_ref[0] = total.astype(bf16)


def body(
    query_proj,
    key_proj,
    value_proj,
    residual,
    norm_gain,
    router_logit,
    expert_ids,
    gate_weight,
    up_weight,
    down_weight,
):
    shard, quarter = query_proj.shape[1:]
    seq, experts = lax.axis_size("seq"), lax.axis_size("exp")
    sid = lax.axis_index("seq").astype(jnp.int32)[None]
    eid = lax.axis_index("exp").astype(jnp.int32)[None]
    fid = lax.axis_index("ff").astype(jnp.int32)[None]
    cap = max(2, 3 * shard // (2 * experts))
    slots = experts * cap
    two = experts == 2
    like = jax.ShapeDtypeStruct

    def far_off(x):
        return pltpu.with_memory_space_constraint(x, pltpu.HBM)

    dma = pltpu.SemaphoreType.DMA
    near = pltpu.VMEM
    kv = kernel(
        pack_body, near((2 * shard, key_proj.shape[2]), bf16), [RAW] * 2, VMEM, 4, scratch=[dma((2,))],
    )(far_off(key_proj), far_off(value_proj))
    kv2 = flip(kv, later=True, seq=2)
    kv1 = flip(kv, later=True, seq=1)
    extras = 2 if two else 1
    query, res, taken, *extra, lit = kernel(
        functools.partial(prep_body, experts, cap),
        (
            near((shard, quarter), bf16),
            near((shard, quarter), bf16),
            near((shard, slots), bf16),
            *[near((EXTRA, quarter), bf16)] * extras,
            near((1, slots), f32),
        ),
        [SMEM] + [RAW] * 5,
        (VMEM,) * (4 + extras),
        8,
        scratch=[near((1, shard), jnp.int32), near((1, shard), f32), near((quarter,), f32), dma((5,))],
    )(eid, far_off(query_proj), far_off(residual), far_off(expert_ids[0, :, 0][None]), far_off(router_logit), far_off(norm_gain))
    kv3 = flip(kv2, seq=1)

    layout = [(0, cap, 0), (cap, cap, 1), (cap, cap, None)] if two else [(0, slots, None)]
    stream, *send = kernel(
        functools.partial(attend_body, HEADS // KVH, seq, extras, layout),
        [near((shard, quarter), bf16)] + [near((n + (0 if e is None else EXTRA), quarter), bf16) for _, n, e in layout],
        [SMEM] + [VMEM] * (3 + seq + extras),
        (VMEM,) * (1 + len(layout)),
        8,
    )(sid, query, res, taken, kv, kv1, kv2, kv3, *extra)

    weights = (gate_weight[0], up_weight[0], down_weight[0])
    tied, send = lax.optimization_barrier((weights, send))
    if two:
        mine, other, bare = send
        sel = join(flip(mine, ff=3), flip(bare, exp=1, ff=3))
        non = join(flip(mine, ff=1), flip(bare, exp=1, ff=1))
        own = [mine, flip(other, exp=1)]
        own_x = [flip(mine, seq=2), flip(other, seq=2, exp=1)]
        far_x = [flip(own_x[0], ff=2), flip(own_x[1], ff=2)]
        one = ((0, 0, cap), (0, cap + EXTRA, cap)), cap
        both = ((0, 0, cap), (1, 0, cap)), cap
        lit_of = ((cap + 3, cap), (cap + 3, cap))
        cut = 2
    else:
        block = lax.all_to_all(send[0], "exp", split_axis=0, concat_axis=0, tiled=True)
        lit = lax.all_to_all(lit[0], "exp", split_axis=0, concat_axis=0, tiled=True)
        lit = jnp.pad(jnp.stack(split(lit)), ((0, 0), (0, quarter - slots)))
        tail = jnp.concatenate([extra[0][:3], lit, extra[0][6:]], axis=0)
        block = jnp.concatenate([block, tail], axis=0)
        own, own_x = [block], [flip(block, seq=2)]
        sel, non = flip(block, ff=3), flip(block, ff=1)
        one = both = ((0, 0, slots),), slots
        far_x = [flip(own_x[0], ff=2)]
        lit_of = ((slots + 3, slots),)
        cut = 1
    partner = [flip(w, seq=1) for w in tied]
    pairs = [w for each in zip(load(weights), load(partner)) for w in each]
    far = flip(sel, ff=1)
    sel_x = flip(sel, seq=2)
    non_x = flip(non, seq=2)

    def lit_in(arrays):
        return [(a, row, n) for a, (row, n) in zip(arrays, lit_of)]

    begun = mlp(fid, [(own, *both, 0), ([sel], *one, 3), ([non], *one, 1)], pairs)
    p0, p1, p2, p3 = mlp(fid, [([far], *one, 2)], pairs, cut, begun, lit_in(own))
    begun = mlp(fid, [(own_x, *both, 0), (far_x, *both, 2), ([sel_x], *one, 3)], pairs)
    o0, o1, o2, o3 = mlp(fid, [([non_x], *one, 1)], pairs, cut, begun, lit_in(own_x))

    back_x = flip(o2, ff=1)
    back = flip(p2, ff=1)
    tot_non = add(p1, flip(o1, seq=2))
    tot_sel = add(p3, back, flip(add(o3, back_x), seq=2))
    if two:
        parts = [
            p0[0], flip(o0[0], seq=2), flip(tot_non[:cap], ff=1), flip(tot_sel[:cap], ff=3),
            flip(p0[1], exp=1), flip(o0[1], seq=2, exp=1),
            flip(tot_non[cap:], exp=1, ff=1), flip(tot_sel[cap:], exp=1, ff=3),
        ]
        shape = (4, 4)
    else:
        parts = add(p0[0], flip(o0[0], seq=2), flip(tot_non, ff=1), flip(tot_sel, ff=3))
        parts = [lax.all_to_all(parts, "exp", split_axis=0, concat_axis=0, tiled=True)]
        shape = (1,)
    return kernel(
        functools.partial(final_body, shape), like((1, shard, quarter), bf16), [VMEM] * (2 + len(parts)), VMEM, 8
    )(stream, taken, *parts)


def solution(mesh):
    placed = (
        P("exp", "seq", "ff"),
        P("exp", "seq", "ff"),
        P("exp", "seq", "ff"),
        P("exp", "seq", "ff"),
        P("ff"),
        P("exp", "seq"),
        P("exp", "seq", None),
        P("exp", None, ("seq", "ff")),
        P("exp", None, ("seq", "ff")),
        P("exp", ("seq", "ff"), None),
    )

    return jax.shard_map(body, mesh=mesh, in_specs=placed, out_specs=P("exp", "seq", "ff"), check_vma=False)
```

```python
import functools
import jax
import jax.numpy as jnp
from jax import lax
from jax.experimental import pallas as pl
from jax.experimental.pallas import tpu as pltpu
from jax.sharding import PartitionSpec as P

HD = 128
HEADS = 20
KVH = 4

floor_score = -1e30
norm_eps = 1e-05
EXTRA = 16
f32 = jnp.float32
bf16 = jnp.bfloat16
VMEM = pl.BlockSpec(memory_space=pltpu.VMEM)
SMEM = pl.BlockSpec(memory_space=pltpu.SMEM)
RAW = pl.BlockSpec(memory_space=pltpu.HBM)


def kernel(body, out, ins, outs, limit, scratch=(), cost=None):
    return pl.pallas_call(
        body,
        out_shape=out,
        in_specs=ins,
        out_specs=outs,
        scratch_shapes=scratch,
        compiler_params=pltpu.CompilerParams(vmem_limit_bytes=limit << 20),
        cost_estimate=cost,
    )


def flip(value, cross=False, later=False, seq=0, exp=0, ff=0):
    axes = ("seq", "exp", "ff")
    sizes = [lax.axis_size(axis) for axis in axes]

    def flat(s, e, f):
        return (s * sizes[1] + e) * sizes[2] + f

    pairs = []
    for s in range(sizes[0]):
        for e in range(sizes[1]):
            for f in range(sizes[2]):
                turn = exp ^ (1 if cross and s % 2 else 0)
                if not later or s < s ^ seq:
                    pairs.append((flat(s, e, f), flat(s ^ seq, e ^ turn, f ^ ff)))
    return lax.ppermute(value, axes, pairs)


def as_column(row):
    n = row.shape[1]
    eye = lax.broadcasted_iota(jnp.int32, (n, n), 0) == lax.broadcasted_iota(jnp.int32, (n, n), 1)
    return jnp.sum(jnp.where(eye, row, 0.0), axis=1, keepdims=True)


def pack_body(k_ref, v_ref, out_ref, sems):
    shard = k_ref.shape[1]
    copies = [
        pltpu.make_async_copy(k_ref.at[0], out_ref.at[pl.ds(0, shard)], sems.at[0]),
        pltpu.make_async_copy(v_ref.at[0], out_ref.at[pl.ds(shard, shard)], sems.at[1]),
    ]
    for c in copies:
        c.start()
    for c in copies:
        c.wait()


def split(value):
    high = value.astype(bf16)
    rest = value - high.astype(f32)
    middle = rest.astype(bf16)
    return [high, middle, (rest - middle.astype(f32)).astype(bf16)]


def prep_body(experts, cap, where_ref, q_in, res_in, ids_in, logit_in, gain_in, q_out, res_out, taken_ref, *refs):
    extra_refs = refs[: 2 if experts == 2 else 1]
    lit_ref, ids_ref, logit_ref, gain_ref, sems = refs[len(extra_refs) :]
    pairs = [(ids_in, ids_ref), (logit_in, logit_ref), (gain_in, gain_ref), (q_in.at[0], q_out), (res_in.at[0], res_out)]
    copies = [pltpu.make_async_copy(x, y, sems.at[i]) for i, (x, y) in enumerate(pairs)]
    for c in copies:
        c.start()
    copies[0].wait()
    shard = ids_ref.shape[1]
    slots = taken_ref.shape[1]
    route = as_column(ids_ref[...].astype(f32)).astype(jnp.int32)
    if experts == 2:
        route = route ^ where_ref[0]
    lanes = lax.broadcasted_iota(jnp.int32, (shard, shard), 1)
    rows = lax.broadcasted_iota(jnp.int32, (shard, shard), 0)
    onehot = (lanes == route).astype(f32)
    below = (rows > lanes).astype(bf16)
    earlier = jnp.dot(below, onehot.astype(bf16), preferred_element_type=f32)
    slot = jnp.sum(earlier * onehot, axis=1, keepdims=True).astype(jnp.int32)
    target = route * cap + slot
    taken = lax.broadcasted_iota(jnp.int32, (shard, slots), 1) == target
    taken_ref[...] = taken.astype(bf16)
    copies[1].wait()
    opened = as_column(1.0 / (1.0 + jnp.exp(-logit_ref[...])))
    lit = jnp.sum(jnp.where(taken, opened, 0.0), axis=0, keepdims=True)
    lit_ref[...] = lit
    copies[2].wait()
    width = gain_ref.shape[0]
    gain = gain_ref[...].reshape(1, width)
    none = [jnp.zeros((1, width), bf16)] * 3
    if experts == 2:
        full = [split(jnp.concatenate([part, jnp.zeros((1, width - cap), f32)], axis=1)) for part in (lit[:, :cap], lit[:, cap:])]
    else:
        full = [none]
    for ref, part, top in zip(extra_refs, full, (split(gain), none)):
        ref[...] = jnp.concatenate([*top, *part, jnp.zeros((EXTRA - 6, width), bf16)], axis=0)
    for c in copies[3:]:
        c.wait()


def attend_body(group, blocks, extras, layout, where_ref, q_ref, res_ref, taken_ref, *refs):
    kv_refs = refs[:blocks]
    extra_refs = refs[blocks : blocks + extras]
    stream_ref = refs[blocks + extras]
    send_refs = refs[blocks + extras + 1 :]
    shard = q_ref.shape[0]
    me = where_ref[0]
    rows = lax.broadcasted_iota(jnp.int32, (shard, shard), 0)
    cols = lax.broadcasted_iota(jnp.int32, (shard, shard), 1)
    nt = (((1,), (1,)), ((), ()))
    pieces = []
    for h in range(q_ref.shape[1] // HD):
        g = h // group
        q = q_ref[:, h * HD : (h + 1) * HD]
        scores = []
        for b in range(blocks):
            s = lax.dot_general(q, kv_refs[b][:shard, g * HD : (g + 1) * HD], nt, preferred_element_type=f32)
            s = s * HD ** (-0.5)
            ok = cols <= rows if b == 0 else cols < jnp.where((me ^ b) < me, shard, 0)
            scores.append(jnp.where(ok, s, floor_score))
        top = jnp.max(functools.reduce(jnp.maximum, scores), axis=1, keepdims=True)
        weights = [jnp.exp(s - top) for s in scores]
        total = jnp.sum(functools.reduce(jnp.add, weights), axis=1, keepdims=True)
        acc = jnp.zeros((shard, HD), f32)
        for b in range(blocks):
            acc += jnp.dot(weights[b].astype(bf16), kv_refs[b][shard:, g * HD : (g + 1) * HD], preferred_element_type=f32)
        pieces.append(acc / total)
    stream = (res_ref[...].astype(f32) + jnp.concatenate(pieces, axis=1)).astype(bf16)
    stream_ref[...] = stream
    tn = (((0,), (0,)), ((), ()))
    send = lax.dot_general(taken_ref[...], stream, tn, preferred_element_type=f32).astype(bf16)
    for ref, (at, rows, extra) in zip(send_refs, layout):
        ref[:rows] = send[at : at + rows]
        if extra:
            own, got = extra_refs[0][...], extra_refs[1][...]
            ref[rows:] = jnp.concatenate([own[:6], got[3:6], own[9:]], axis=0)


def joined(refs, spans):
    parts = [refs[i][at : at + rows] for i, at, rows in spans]
    return parts[0] if len(parts) == 1 else jnp.concatenate(parts, axis=0)


def whole(ref, row, width):
    return sum(ref[row + i : row + i + 1, :width].astype(f32) for i in range(3))


def load_body(*refs):
    n = len(refs) // 2
    sems = refs[-1]
    copies = [pltpu.make_async_copy(refs[i], refs[n + i], sems.at[i]) for i in range(n)]
    for c in copies:
        c.start()
    for c in copies:
        c.wait()


def load(arrays):
    n = len(arrays)
    return kernel(
        load_body, [pltpu.VMEM(a.shape, a.dtype) for a in arrays], [RAW] * n, [VMEM] * n, 4,
        scratch=[pltpu.SemaphoreType.DMA((n,))],
    )(*[pltpu.with_memory_space_constraint(a, pltpu.HBM) for a in arrays])


def join_body(keep_ref, got_ref, out_ref):
    cap = got_ref.shape[0]
    out_ref[:cap] = keep_ref[:cap]
    out_ref[cap : 2 * cap] = got_ref[...]
    out_ref[2 * cap :] = keep_ref[cap:]


def mlp_body(spec, lit_of, begun, where_ref, *refs):
    refs = list(refs)
    acc_in = [refs.pop(0) for _ in range(3)] if begun else None
    blocks = [([refs.pop(0) for _ in range(n)], spans, gain, i) for n, spans, gain, i in spec]
    lits = [refs.pop(0) for _ in lit_of]
    gates, ups = ([refs.pop(0) for _ in range(2)] for _ in range(2))
    mine = where_ref[0]
    g, u, squares = ([None, None], [None, None], None)
    if begun:
        hidden = gates[0].shape[1]
        g = [acc_in[0][:, k * hidden : (k + 1) * hidden] for k in range(2)]
        u = [acc_in[1][:, k * hidden : (k + 1) * hidden] for k in range(2)]
        squares = acc_in[2][:, :1]

    def plus(x, y):
        return y if x is None else x + y

    for arrays, spans, gain_row, i in blocks:
        at = mine ^ i
        wide = joined(arrays, spans).astype(f32)
        quarter = wide.shape[1]
        squares = plus(squares, jnp.sum(wide * wide, axis=1, keepdims=True))
        x = (wide * whole(arrays[0], gain_row, quarter)).astype(bf16)
        part = pl.ds(pl.multiple_of(at * quarter, quarter), quarter)
        for k in range(2):
            g[k] = plus(g[k], jnp.dot(x, gates[k][part, :], preferred_element_type=f32))
            u[k] = plus(u[k], jnp.dot(x, ups[k][part, :], preferred_element_type=f32))
    if not lit_of:
        g_ref, u_ref, s_ref = refs
        g_ref[...] = jnp.concatenate(g, axis=1)
        u_ref[...] = jnp.concatenate(u, axis=1)
        s_ref[...] = jnp.broadcast_to(squares, s_ref.shape)
        return
    downs = [refs.pop(0) for _ in range(2)]
    outs = refs
    rows, quarter = outs[0].shape
    opened = [as_column(whole(ref, row, n)) for ref, (row, n) in zip(lits, lit_of)]
    opened = opened[0] if len(opened) == 1 else jnp.concatenate(opened, axis=0)
    factor = lax.rsqrt(squares / (4 * quarter) + norm_eps) * opened
    act = []
    for k in range(2):
        gate, up = g[k] * factor, u[k] * factor
        act.append((gate / (1.0 + jnp.exp(-gate)) * up).astype(bf16))
    for i in (3, 1, 2, 0):
        at = mine ^ i
        part = pl.ds(pl.multiple_of(at * quarter, quarter), quarter)
        y = jnp.dot(act[0], downs[0][:, part], preferred_element_type=f32)
        y += jnp.dot(act[1], downs[1][:, part], preferred_element_type=f32)
        y = y.astype(bf16)
        if i < 3 or len(outs) == 4:
            outs[i][...] = y
        else:
            outs[3][...] = y[: rows // 2]
            outs[4][...] = y[rows // 2 :]


def mlp(mine, blocks, weights, begun=None, lits=(), halve=False):
    spec = [(len(arrays), spans, gain, i) for arrays, spans, gain, i in blocks]
    rows, quarter = sum(n for _, _, n in blocks[0][1]), blocks[0][0][0].shape[1]
    flat = [*(begun or ()), *[a for arrays, *_ in blocks for a in arrays], *[a for a, _, _ in lits]]
    hidden = weights[0].shape[1]
    flops = 2 * rows * quarter * len(blocks) * hidden * 4
    if lits:
        out = [pltpu.VMEM((rows, quarter), bf16)] * 3
        out += [pltpu.VMEM((rows // 2, quarter), bf16)] * 2 if halve else out[:1]
        flops += 2 * rows * quarter * 4 * hidden * 2
    else:
        out = [pltpu.VMEM((rows, 2 * hidden), f32)] * 2 + [pltpu.VMEM((rows, HD), f32)]
        weights = weights[:4]
    weights = [pltpu.with_memory_space_constraint(w, pltpu.VMEM) for w in weights]
    return kernel(
        functools.partial(mlp_body, spec, [(row, n) for _, row, n in lits], begun is not None),
        out,
        [SMEM] + [VMEM] * (len(flat) + len(weights)),
        [VMEM] * len(out),
        12,
        cost=pl.CostEstimate(flops=flops, bytes_accessed=8 << 20, transcendentals=0),
    )(mine, *flat, *weights)


def add(*parts):
    total = parts[0].astype(f32)
    for part in parts[1:]:
        total = total + part.astype(f32)
    return total.astype(bf16)


def sum_body(tops, *refs):
    out_ref = refs[-1]
    rows = out_ref.shape[0]
    total = refs[0][tops[0] : tops[0] + rows].astype(f32)
    for ref, top in zip(refs[1:-1], tops[1:]):
        total += ref[top : top + rows].astype(f32)
    out_ref[...] = total.astype(bf16)


def sum_rows(rows, *parts):
    shape = (rows, parts[0][0].shape[1])
    return kernel(
        functools.partial(sum_body, [top for _, top in parts]), pltpu.VMEM(shape, bf16), [VMEM] * len(parts), VMEM, 4
    )(*[a for a, _ in parts])


def final_body(shape, stream_ref, taken_ref, *refs):
    refs = list(refs)
    out_ref = refs.pop()
    total = stream_ref[...].astype(f32)
    at = 0
    for n in shape:
        part = refs.pop(0)[...]
        for _ in range(n - 1):
            part = (part.astype(f32) + refs.pop(0)[...].astype(f32)).astype(bf16)
        rows = part.shape[0]
        total += jnp.dot(taken_ref[:, at : at + rows], part, preferred_element_type=f32)
        at += rows
    out_ref[0] = total.astype(bf16)


def body(
    query_proj,
    key_proj,
    value_proj,
    residual,
    norm_gain,
    router_logit,
    expert_ids,
    gate_weight,
    up_weight,
    down_weight,
):
    shard, quarter = query_proj.shape[1:]
    seq, experts = lax.axis_size("seq"), lax.axis_size("exp")
    sid = lax.axis_index("seq").astype(jnp.int32)[None]
    eid = lax.axis_index("exp").astype(jnp.int32)[None] ^ (sid & 1)
    fid = lax.axis_index("ff").astype(jnp.int32)[None]
    cap = max(2, 3 * shard // (2 * experts))
    slots = experts * cap
    two = experts == 2
    like = jax.ShapeDtypeStruct

    def far_off(x):
        return pltpu.with_memory_space_constraint(x, pltpu.HBM)

    dma = pltpu.SemaphoreType.DMA
    near = pltpu.VMEM
    kv = kernel(
        pack_body, near((2 * shard, key_proj.shape[2]), bf16), [RAW] * 2, VMEM, 4, scratch=[dma((2,))],
    )(far_off(key_proj), far_off(value_proj))
    kv2 = flip(kv, later=True, seq=2)
    kv1 = flip(kv, later=True, seq=1)
    kv3 = flip(kv2, seq=1)
    extras = 2 if two else 1
    query, res, taken, *extra, lit = kernel(
        functools.partial(prep_body, experts, cap),
        (
            near((shard, quarter), bf16),
            near((shard, quarter), bf16),
            near((shard, slots), bf16),
            *[near((EXTRA, quarter), bf16)] * extras,
            near((1, slots), f32),
        ),
        [SMEM] + [RAW] * 5,
        (VMEM,) * (4 + extras),
        8,
        scratch=[near((1, shard), jnp.int32), near((1, shard), f32), near((quarter,), f32), dma((5,))],
    )(eid, far_off(query_proj), far_off(residual), far_off(expert_ids[0, :, 0][None]), far_off(router_logit), far_off(norm_gain))

    layout = [(0, cap, True), (cap, cap, False)] if two else [(0, slots, False)]
    if two:
        extra[1] = flip(extra[1], seq=1)
    stream, *send = kernel(
        functools.partial(attend_body, HEADS // KVH, seq, extras, layout),
        [near((shard, quarter), bf16)] + [near((n + (EXTRA if e else 0), quarter), bf16) for _, n, e in layout],
        [SMEM] + [VMEM] * (3 + seq + extras),
        (VMEM,) * (1 + len(layout)),
        8,
    )(sid, query, res, taken, kv, kv1, kv2, kv3, *extra)

    rows = 2 * cap if two else slots
    if two:
        got = flip(send[1], seq=1)
        halves = [send[0], got]
        block = kernel(join_body, near((rows + EXTRA, quarter), bf16), [VMEM] * 2, VMEM, 4)(*halves)
        lit_of = ((rows + 3, cap), (rows + 6, cap))
        spans, gain_row = ((0, 0, cap), (1, 0, cap)), cap
    else:
        block = lax.all_to_all(send[0], "exp", split_axis=0, concat_axis=0, tiled=True)
        lit = lax.all_to_all(lit[0], "exp", split_axis=0, concat_axis=0, tiled=True)
        lit = jnp.pad(jnp.stack(split(lit)), ((0, 0), (0, quarter - slots)))
        block = jnp.concatenate([block, extra[0][:3], lit, extra[0][6:]], axis=0)
        halves = [block]
        lit_of = ((rows + 3, slots),)
        spans, gain_row = ((0, 0, rows),), rows

    def each(arrays, *args, **bits):
        return [flip(a, *args, **bits) for a in arrays]

    weights = (gate_weight[0], up_weight[0], down_weight[0])
    sel = each(halves, two, ff=2)
    non = flip(block, two, ff=1)
    own_x = flip(block, two, seq=2)
    own = flip(block, two) if two else block
    partner = each(weights, seq=1)
    pairs = [w for both in zip(load(weights), load(partner)) for w in both]
    far = each(sel, ff=1)
    sel_x = each(sel, seq=2)
    non_x = flip(non, seq=2)
    far_x = each(sel_x, ff=1)

    def blocks(*parts):
        return [([a], ((0, 0, rows),), rows, i) if not isinstance(a, list) else (a, spans, gain_row, i) for a, i in parts]

    def lit_in(array):
        return [(array, row, n) for row, n in lit_of]

    begun = mlp(fid, blocks((own, 0), (sel, 2), (non, 1)), pairs)
    p0, p1, p2, p3 = mlp(fid, blocks((far, 3)), pairs, begun, lit_in(own))
    begun = mlp(fid, blocks((own_x, 0), (sel_x, 2), (non_x, 1)), pairs)
    o0, o1, o2, *o3 = mlp(fid, blocks((far_x, 3)), pairs, begun, lit_in(own_x), two)

    part = cap if two else slots
    order = range(len(o3))
    back_x = each(o3, ff=1)
    back = flip(p3, ff=1)
    over = each([sum_rows(part, (o2, i * part), (back_x[i], 0)) for i in order], seq=2)
    last = [sum_rows(part, (p2, i * part), (back, i * part), (over[i], 0)) for i in order]
    last = each(last, two, ff=2)
    tot_non = sum_rows(rows, (p1, 0), (flip(o1, seq=2), 0))
    home = flip(p0, two) if two else p0
    most = [home, flip(o0, two, seq=2), flip(tot_non, two, ff=1)]
    most = [sum_rows(part, *[(a, i * part) for a in most]) for i in order]
    if two:
        parts = [most[0], last[0], flip(most[1], seq=1), flip(last[1], seq=1)]
        shape = (2, 2)
    else:
        parts = [lax.all_to_all(add(most[0], last[0]), "exp", split_axis=0, concat_axis=0, tiled=True)]
        shape = (1,)
    return kernel(
        functools.partial(final_body, shape), like((1, shard, quarter), bf16), [VMEM] * (2 + len(parts)), VMEM, 8
    )(stream, taken, *parts)


def solution(mesh):
    placed = (
        P("exp", "seq", "ff"),
        P("exp", "seq", "ff"),
        P("exp", "seq", "ff"),
        P("exp", "seq", "ff"),
        P("ff"),
        P("exp", "seq"),
        P("exp", "seq", None),
        P("exp", None, ("seq", "ff")),
        P("exp", None, ("seq", "ff")),
        P("exp", ("seq", "ff"), None),
    )

    return jax.shard_map(body, mesh=mesh, in_specs=placed, out_specs=P("exp", "seq", "ff"), check_vma=False)
```

```python
import functools
import jax
import jax.numpy as jnp
from jax import lax
from jax.experimental import pallas as pl
from jax.experimental.pallas import tpu as pltpu
from jax.sharding import PartitionSpec as P

HD = 128
HEADS = 20
KVH = 4

floor_score = -1e30
norm_eps = 1e-05
EXTRA = 8
f32 = jnp.float32
bf16 = jnp.bfloat16
VMEM = pl.BlockSpec(memory_space=pltpu.VMEM)
SMEM = pl.BlockSpec(memory_space=pltpu.SMEM)
RAW = pl.BlockSpec(memory_space=pltpu.HBM)


def kernel(body, out, ins, outs, limit, scratch=(), cost=None):
    return pl.pallas_call(
        body,
        out_shape=out,
        in_specs=ins,
        out_specs=outs,
        scratch_shapes=scratch,
        compiler_params=pltpu.CompilerParams(vmem_limit_bytes=limit << 20),
        cost_estimate=cost,
    )


def flip(value, cross=False, later=False, seq=0, exp=0, ff=0):
    axes = ("seq", "exp", "ff")
    sizes = [lax.axis_size(axis) for axis in axes]

    def flat(s, e, f):
        return (s * sizes[1] + e) * sizes[2] + f

    pairs = []
    for s in range(sizes[0]):
        for e in range(sizes[1]):
            for f in range(sizes[2]):
                turn = exp ^ (1 if cross and s % 2 else 0)
                if not later or s < s ^ seq:
                    pairs.append((flat(s, e, f), flat(s ^ seq, e ^ turn, f ^ ff)))
    return lax.ppermute(value, axes, pairs)


def as_column(row):
    n = row.shape[1]
    eye = lax.broadcasted_iota(jnp.int32, (n, n), 0) == lax.broadcasted_iota(jnp.int32, (n, n), 1)
    return jnp.sum(jnp.where(eye, row, 0.0), axis=1, keepdims=True)


def pack_body(k_ref, v_ref, out_ref, sems):
    shard = k_ref.shape[1]
    copies = [
        pltpu.make_async_copy(k_ref.at[0], out_ref.at[pl.ds(0, shard)], sems.at[0]),
        pltpu.make_async_copy(v_ref.at[0], out_ref.at[pl.ds(shard, shard)], sems.at[1]),
    ]
    for c in copies:
        c.start()
    for c in copies:
        c.wait()


def split(value):
    high = value.astype(bf16)
    rest = value - high.astype(f32)
    middle = rest.astype(bf16)
    return [high, middle, (rest - middle.astype(f32)).astype(bf16)]


def prep_body(experts, ff, cap, where_ref, q_in, res_in, ids_in, logit_in, gain_in, q_out, res_out, taken_ref, *refs):
    extra_refs = refs[: 2 if experts == 2 else 1]
    lit_ref, ids_ref, logit_ref, gain_ref, sems = refs[len(extra_refs) :]
    pairs = [(ids_in, ids_ref), (logit_in, logit_ref), (gain_in, gain_ref), (q_in.at[0], q_out), (res_in.at[0], res_out)]
    copies = [pltpu.make_async_copy(x, y, sems.at[i]) for i, (x, y) in enumerate(pairs)]
    for c in copies:
        c.start()
    copies[0].wait()
    shard = ids_ref.shape[1]
    slots = taken_ref.shape[1]
    route = as_column(ids_ref[...].astype(f32)).astype(jnp.int32)
    if experts == 2:
        route = route ^ (where_ref[0] // ff % experts) ^ (where_ref[0] // (ff * experts) & 1)
    lanes = lax.broadcasted_iota(jnp.int32, (shard, shard), 1)
    rows = lax.broadcasted_iota(jnp.int32, (shard, shard), 0)
    onehot = (lanes == route).astype(f32)
    below = (rows > lanes).astype(bf16)
    earlier = jnp.dot(below, onehot.astype(bf16), preferred_element_type=f32)
    slot = jnp.sum(earlier * onehot, axis=1, keepdims=True).astype(jnp.int32)
    target = route * cap + slot
    taken = lax.broadcasted_iota(jnp.int32, (shard, slots), 1) == target
    taken_ref[...] = taken.astype(bf16)
    copies[1].wait()
    opened = as_column(1.0 / (1.0 + jnp.exp(-logit_ref[...])))
    lit = jnp.sum(jnp.where(taken, opened, 0.0), axis=0, keepdims=True)
    lit_ref[...] = lit
    copies[2].wait()
    width = gain_ref.shape[0]
    gain = gain_ref[...].reshape(1, width)
    none = [jnp.zeros((1, width), bf16)] * 3
    if experts == 2:
        full = [split(jnp.concatenate([part, jnp.zeros((1, width - cap), f32)], axis=1)) for part in (lit[:, :cap], lit[:, cap:])]
    else:
        full = [none]
    for ref, part, top in zip(extra_refs, full, (split(gain), none)):
        ref[...] = jnp.concatenate([*top, *part, jnp.zeros((EXTRA - 6, width), bf16)], axis=0)
    for c in copies[3:]:
        c.wait()


def attend_body(group, blocks, plane, layout, where_ref, q_ref, res_ref, taken_ref, *refs):
    kv_refs = refs[:blocks]
    extra_refs = refs[blocks : blocks + 1]
    stream_ref = refs[blocks + 1]
    send_refs = refs[blocks + 2 :]
    shard = q_ref.shape[0]
    me = where_ref[0] // plane
    rows = lax.broadcasted_iota(jnp.int32, (shard, shard), 0)
    cols = lax.broadcasted_iota(jnp.int32, (shard, shard), 1)
    nt = (((1,), (1,)), ((), ()))
    pieces = []
    for h in range(q_ref.shape[1] // HD):
        g = h // group
        q = q_ref[:, h * HD : (h + 1) * HD]
        scores = []
        for b in range(blocks):
            s = lax.dot_general(q, kv_refs[b][:shard, g * HD : (g + 1) * HD], nt, preferred_element_type=f32)
            s = s * HD ** (-0.5)
            ok = cols <= rows if b == 0 else cols < jnp.where((me ^ b) < me, shard, 0)
            scores.append(jnp.where(ok, s, floor_score))
        top = jnp.max(functools.reduce(jnp.maximum, scores), axis=1, keepdims=True)
        weights = [jnp.exp(s - top) for s in scores]
        total = jnp.sum(functools.reduce(jnp.add, weights), axis=1, keepdims=True)
        acc = jnp.zeros((shard, HD), f32)
        for b in range(blocks):
            acc += jnp.dot(weights[b].astype(bf16), kv_refs[b][shard:, g * HD : (g + 1) * HD], preferred_element_type=f32)
        pieces.append(acc / total)
    stream = (res_ref[...].astype(f32) + jnp.concatenate(pieces, axis=1)).astype(bf16)
    stream_ref[...] = stream
    tn = (((0,), (0,)), ((), ()))
    send = lax.dot_general(taken_ref[...], stream, tn, preferred_element_type=f32).astype(bf16)
    for ref, (at, rows, extra) in zip(send_refs, layout):
        ref[:rows] = send[at : at + rows]
        if extra:
            ref[rows:] = extra_refs[0][...]


def joined(refs, spans):
    parts = [refs[i][at : at + rows] for i, at, rows in spans]
    return parts[0] if len(parts) == 1 else jnp.concatenate(parts, axis=0)


def whole(ref, row, lane, width):
    return sum(ref[row + i : row + i + 1, lane : lane + width].astype(f32) for i in range(3))


def load_body(*refs):
    n = len(refs) // 2
    sems = refs[-1]
    copies = [pltpu.make_async_copy(refs[i], refs[n + i], sems.at[i]) for i in range(n)]
    for c in copies:
        c.start()
    for c in copies:
        c.wait()


def load(arrays):
    n = len(arrays)
    return kernel(
        load_body, [pltpu.VMEM(a.shape, a.dtype) for a in arrays], [RAW] * n, [VMEM] * n, 4,
        scratch=[pltpu.SemaphoreType.DMA((n,))],
    )(*[pltpu.with_memory_space_constraint(a, pltpu.HBM) for a in arrays])


def join_body(keep_ref, got_ref, extra_ref, out_ref):
    cap = got_ref.shape[0]
    out_ref[:cap] = keep_ref[:cap]
    out_ref[cap : 2 * cap] = got_ref[...]
    own, got = keep_ref[cap:], extra_ref[...]
    both = jnp.concatenate([own[3:6, :HD], got[3:6, :HD], own[3:6, 2 * HD :]], axis=1)
    out_ref[2 * cap :] = jnp.concatenate([own[:3], both, own[6:]], axis=0)


def mlp_body(ff, spec, lit_of, begun, where_ref, *refs):
    refs = list(refs)
    acc_in = [refs.pop(0) for _ in range(3)] if begun else None
    blocks = [([refs.pop(0) for _ in range(n)], spans, gain, i) for n, spans, gain, i in spec]
    lits = [refs.pop(0) for _ in lit_of]
    gates, ups = ([refs.pop(0) for _ in range(2)] for _ in range(2))
    mine = lax.rem(where_ref[0], ff)
    g, u, squares = ([None, None], [None, None], None)
    if begun:
        hidden = gates[0].shape[1]
        g = [acc_in[0][:, k * hidden : (k + 1) * hidden] for k in range(2)]
        u = [acc_in[1][:, k * hidden : (k + 1) * hidden] for k in range(2)]
        squares = acc_in[2][:, :1]

    def plus(x, y):
        return y if x is None else x + y

    for arrays, spans, gain_row, i in blocks:
        at = mine ^ i
        wide = joined(arrays, spans).astype(f32)
        quarter = wide.shape[1]
        squares = plus(squares, jnp.sum(wide * wide, axis=1, keepdims=True))
        x = (wide * whole(arrays[0], gain_row, 0, quarter)).astype(bf16)
        part = pl.ds(pl.multiple_of(at * quarter, quarter), quarter)
        for k in range(2):
            g[k] = plus(g[k], jnp.dot(x, gates[k][part, :], preferred_element_type=f32))
            u[k] = plus(u[k], jnp.dot(x, ups[k][part, :], preferred_element_type=f32))
    if not lit_of:
        g_ref, u_ref, s_ref = refs
        g_ref[...] = jnp.concatenate(g, axis=1)
        u_ref[...] = jnp.concatenate(u, axis=1)
        s_ref[...] = jnp.broadcast_to(squares, s_ref.shape)
        return
    downs = [refs.pop(0) for _ in range(2)]
    outs = refs
    rows, quarter = outs[0].shape
    opened = [as_column(whole(ref, *place)) for ref, place in zip(lits, lit_of)]
    opened = opened[0] if len(opened) == 1 else jnp.concatenate(opened, axis=0)
    factor = lax.rsqrt(squares / (4 * quarter) + norm_eps) * opened
    act = []
    for k in range(2):
        gate, up = g[k] * factor, u[k] * factor
        act.append((gate / (1.0 + jnp.exp(-gate)) * up).astype(bf16))
    for i in (3, 1, 2, 0):
        at = mine ^ i
        part = pl.ds(pl.multiple_of(at * quarter, quarter), quarter)
        y = jnp.dot(act[0], downs[0][:, part], preferred_element_type=f32)
        y += jnp.dot(act[1], downs[1][:, part], preferred_element_type=f32)
        y = y.astype(bf16)
        if i < 3 or len(outs) == 4:
            outs[i][...] = y
        else:
            outs[3][...] = y[: rows // 2]
            outs[4][...] = y[rows // 2 :]


def mlp(mine, blocks, weights, begun=None, lits=(), halve=False):
    spec = [(len(arrays), spans, gain, i) for arrays, spans, gain, i in blocks]
    rows, quarter = sum(n for _, _, n in blocks[0][1]), blocks[0][0][0].shape[1]
    flat = [*(begun or ()), *[a for arrays, *_ in blocks for a in arrays], *[a for a, *_ in lits]]
    hidden = weights[0].shape[1]
    flops = 2 * rows * quarter * len(blocks) * hidden * 4
    if lits:
        out = [pltpu.VMEM((rows, quarter), bf16)] * 3
        out += [pltpu.VMEM((rows // 2, quarter), bf16)] * 2 if halve else out[:1]
        flops += 2 * rows * quarter * 4 * hidden * 2
    else:
        out = [pltpu.VMEM((rows, 2 * hidden), f32)] * 2 + [pltpu.VMEM((rows, HD), f32)]
        weights = weights[:4]
    weights = [pltpu.with_memory_space_constraint(w, pltpu.VMEM) for w in weights]
    return kernel(
        functools.partial(mlp_body, lax.axis_size("ff"), spec, [tuple(place) for _, *place in lits], begun is not None),
        out,
        [SMEM] + [VMEM] * (len(flat) + len(weights)),
        [VMEM] * len(out),
        12,
        cost=pl.CostEstimate(flops=flops, bytes_accessed=8 << 20, transcendentals=0),
    )(mine, *flat, *weights)


def add(*parts):
    total = parts[0].astype(f32)
    for part in parts[1:]:
        total = total + part.astype(f32)
    return total.astype(bf16)


def sum_body(tops, *refs):
    out_ref = refs[-1]
    rows = out_ref.shape[0]
    total = refs[0][tops[0] : tops[0] + rows].astype(f32)
    for ref, top in zip(refs[1:-1], tops[1:]):
        total += ref[top : top + rows].astype(f32)
    out_ref[...] = total.astype(bf16)


def sum_rows(rows, *parts):
    shape = (rows, parts[0][0].shape[1])
    return kernel(
        functools.partial(sum_body, [top for _, top in parts]), pltpu.VMEM(shape, bf16), [VMEM] * len(parts), VMEM, 4
    )(*[a for a, _ in parts])


def final_body(shape, stream_ref, taken_ref, *refs):
    refs = list(refs)
    out_ref = refs.pop()
    total = stream_ref[...].astype(f32)
    at = 0
    for n in shape:
        part = refs.pop(0)[...]
        for _ in range(n - 1):
            part = (part.astype(f32) + refs.pop(0)[...].astype(f32)).astype(bf16)
        rows = part.shape[0]
        total += jnp.dot(taken_ref[:, at : at + rows], part, preferred_element_type=f32)
        at += rows
    out_ref[0] = total.astype(bf16)


def body(
    query_proj,
    key_proj,
    value_proj,
    residual,
    norm_gain,
    router_logit,
    expert_ids,
    gate_weight,
    up_weight,
    down_weight,
):
    shard, quarter = query_proj.shape[1:]
    seq, experts = lax.axis_size("seq"), lax.axis_size("exp")
    ff = lax.axis_size("ff")
    place = lax.axis_index(("seq", "exp", "ff")).astype(jnp.int32)[None]
    cap = max(2, 3 * shard // (2 * experts))
    slots = experts * cap
    two = experts == 2
    like = jax.ShapeDtypeStruct

    def far_off(x):
        return pltpu.with_memory_space_constraint(x, pltpu.HBM)

    dma = pltpu.SemaphoreType.DMA
    near = pltpu.VMEM
    kv = kernel(
        pack_body, near((2 * shard, key_proj.shape[2]), bf16), [RAW] * 2, VMEM, 4, scratch=[dma((2,))],
    )(far_off(key_proj), far_off(value_proj))
    kv2 = flip(kv, later=True, seq=2)
    kv1 = flip(kv, later=True, seq=1)
    kv3 = flip(kv2, seq=1)
    extras = 2 if two else 1
    query, res, taken, *extra, lit = kernel(
        functools.partial(prep_body, experts, ff, cap),
        (
            near((shard, quarter), bf16),
            near((shard, quarter), bf16),
            near((shard, slots), bf16),
            *[near((EXTRA, quarter), bf16)] * extras,
            near((1, slots), f32),
        ),
        [SMEM] + [RAW] * 5,
        (VMEM,) * (4 + extras),
        8,
        scratch=[near((1, shard), jnp.int32), near((1, shard), f32), near((quarter,), f32), dma((5,))],
    )(place, far_off(query_proj), far_off(residual), far_off(expert_ids[0, :, 0][None]), far_off(router_logit), far_off(norm_gain))

    layout = [(0, cap, True), (cap, cap, False)] if two else [(0, slots, False)]
    stream, *send = kernel(
        functools.partial(attend_body, HEADS // KVH, seq, experts * ff, layout),
        [near((shard, quarter), bf16)] + [near((n + (EXTRA if e else 0), quarter), bf16) for _, n, e in layout],
        [SMEM] + [VMEM] * (4 + seq),
        (VMEM,) * (1 + len(layout)),
        8,
    )(place, query, res, taken, kv, kv1, kv2, kv3, extra[0])

    rows = 2 * cap if two else slots
    if two:
        got = flip(send[1], seq=1)
        halves = [send[0], got]
        block = kernel(join_body, near((rows + EXTRA, quarter), bf16), [VMEM] * 3, VMEM, 4)(*halves, flip(extra[1], seq=1))
        lit_of = ((rows + 3, 0, cap), (rows + 3, HD, cap))
        spans, gain_row = ((0, 0, cap), (1, 0, cap)), cap
    else:
        block = lax.all_to_all(send[0], "exp", split_axis=0, concat_axis=0, tiled=True)
        lit = lax.all_to_all(lit[0], "exp", split_axis=0, concat_axis=0, tiled=True)
        lit = jnp.pad(jnp.stack(split(lit)), ((0, 0), (0, quarter - slots)))
        block = jnp.concatenate([block, extra[0][:3], lit, extra[0][6:]], axis=0)
        halves = [block]
        lit_of = ((rows + 3, 0, slots),)
        spans, gain_row = ((0, 0, rows),), rows

    def each(arrays, *args, **bits):
        return [flip(a, *args, **bits) for a in arrays]

    weights = (gate_weight[0], up_weight[0], down_weight[0])
    sel = each(halves, two, ff=2)
    non = flip(block, two, ff=1)
    own_x = flip(block, two, seq=2)
    own = flip(block, two) if two else block
    partner = each(weights, seq=1)
    pairs = [w for both in zip(load(weights), partner) for w in both]
    far = each(sel, ff=1)
    sel_x = each(sel, seq=2)
    non_x = flip(non, seq=2)
    far_x = each(sel_x, ff=1)

    def blocks(*parts):
        return [([a], ((0, 0, rows),), rows, i) if not isinstance(a, list) else (a, spans, gain_row, i) for a, i in parts]

    def lit_in(array):
        return [(array, *place) for place in lit_of]

    begun = mlp(place, blocks((own, 0), (sel, 2), (non, 1)), pairs)
    p0, p1, p2, *p3 = mlp(place, blocks((far, 3)), pairs, begun, lit_in(own), two)
    begun = mlp(place, blocks((own_x, 0), (sel_x, 2), (non_x, 1)), pairs)
    o0, o1, o2, *o3 = mlp(place, blocks((far_x, 3)), pairs, begun, lit_in(own_x), two)

    part = cap if two else slots
    order = range(len(o3))
    back_x = each(o3, ff=1)
    back = each(p3, ff=1)
    over = each([sum_rows(part, (o2, i * part), (back_x[i], 0)) for i in order], seq=2)
    last = [sum_rows(part, (p2, i * part), (back[i], 0), (over[i], 0)) for i in order]
    last = each(last, two, ff=2)
    tot_non = sum_rows(rows, (p1, 0), (flip(o1, seq=2), 0))
    home = flip(p0, two) if two else p0
    most = [home, flip(o0, two, seq=2), flip(tot_non, two, ff=1)]
    most = [sum_rows(part, *[(a, i * part) for a in most]) for i in order]
    if two:
        parts = [most[0], last[0], flip(most[1], seq=1), flip(last[1], seq=1)]
        shape = (2, 2)
    else:
        parts = [lax.all_to_all(add(most[0], last[0]), "exp", split_axis=0, concat_axis=0, tiled=True)]
        shape = (1,)
    return kernel(
        functools.partial(final_body, shape), like((1, shard, quarter), bf16), [VMEM] * (2 + len(parts)), VMEM, 8
    )(stream, taken, *parts)


def solution(mesh):
    placed = (
        P("exp", "seq", "ff"),
        P("exp", "seq", "ff"),
        P("exp", "seq", "ff"),
        P("exp", "seq", "ff"),
        P("ff"),
        P("exp", "seq"),
        P("exp", "seq", None),
        P("exp", None, ("seq", "ff")),
        P("exp", None, ("seq", "ff")),
        P("exp", ("seq", "ff"), None),
    )

    return jax.shard_map(body, mesh=mesh, in_specs=placed, out_specs=P("exp", "seq", "ff"), check_vma=False)
```

```python
import functools
import jax
import jax.numpy as jnp
from jax import lax
from jax.experimental import pallas as pl
from jax.experimental.pallas import tpu as pltpu
from jax.sharding import PartitionSpec as P

HD = 128
HEADS = 20
KVH = 4

floor_score = -1e30
norm_eps = 1e-05
EXTRA = 8
f32 = jnp.float32
bf16 = jnp.bfloat16
VMEM = pl.BlockSpec(memory_space=pltpu.VMEM)
SMEM = pl.BlockSpec(memory_space=pltpu.SMEM)
RAW = pl.BlockSpec(memory_space=pltpu.HBM)


def kernel(body, out, ins, outs, limit, scratch=(), cost=None):
    return pl.pallas_call(
        body,
        out_shape=out,
        in_specs=ins,
        out_specs=outs,
        scratch_shapes=scratch,
        compiler_params=pltpu.CompilerParams(vmem_limit_bytes=limit << 20),
        cost_estimate=cost,
    )


def flip(value, cross=False, later=None, seq=0, exp=0, ff=0):
    axes = ("seq", "exp", "ff")
    sizes = [lax.axis_size(axis) for axis in axes]

    def flat(s, e, f):
        return (s * sizes[1] + e) * sizes[2] + f

    pairs = []
    for s in range(sizes[0]):
        for e in range(sizes[1]):
            for f in range(sizes[2]):
                turn = exp ^ (1 if cross and s % 2 else 0)
                if later is None or s ^ seq ^ later < s ^ seq:
                    pairs.append((flat(s, e, f), flat(s ^ seq, e ^ turn, f ^ ff)))
    return lax.ppermute(value, axes, pairs)


def as_column(row):
    n = row.shape[1]
    eye = lax.broadcasted_iota(jnp.int32, (n, n), 0) == lax.broadcasted_iota(jnp.int32, (n, n), 1)
    return jnp.sum(jnp.where(eye, row, 0.0), axis=1, keepdims=True)


def pack_body(k_ref, v_ref, out_ref, sems):
    shard = k_ref.shape[1]
    copies = [
        pltpu.make_async_copy(k_ref.at[0], out_ref.at[pl.ds(0, shard)], sems.at[0]),
        pltpu.make_async_copy(v_ref.at[0], out_ref.at[pl.ds(shard, shard)], sems.at[1]),
    ]
    for c in copies:
        c.start()
    for c in copies:
        c.wait()


def split(value):
    high = value.astype(bf16)
    rest = value - high.astype(f32)
    middle = rest.astype(bf16)
    return [high, middle, (rest - middle.astype(f32)).astype(bf16)]


def prep_body(experts, ff, cap, where_ref, q_in, res_in, ids_in, logit_in, gain_in, q_out, res_out, taken_ref, *refs):
    extra_refs = refs[: 2 if experts == 2 else 1]
    lit_ref, ids_ref, logit_ref, gain_ref, sems = refs[len(extra_refs) :]
    pairs = [(ids_in, ids_ref), (logit_in, logit_ref), (gain_in, gain_ref), (q_in.at[0], q_out), (res_in.at[0], res_out)]
    copies = [pltpu.make_async_copy(x, y, sems.at[i]) for i, (x, y) in enumerate(pairs)]
    for c in copies:
        c.start()
    copies[0].wait()
    shard = ids_ref.shape[1]
    slots = taken_ref.shape[1]
    route = as_column(ids_ref[...].astype(f32)).astype(jnp.int32)
    if experts == 2:
        route = route ^ (where_ref[0] // ff % experts) ^ (where_ref[0] // (ff * experts) & 1)
    lanes = lax.broadcasted_iota(jnp.int32, (shard, shard), 1)
    rows = lax.broadcasted_iota(jnp.int32, (shard, shard), 0)
    onehot = (lanes == route).astype(f32)
    below = (rows > lanes).astype(bf16)
    earlier = jnp.dot(below, onehot.astype(bf16), preferred_element_type=f32)
    slot = jnp.sum(earlier * onehot, axis=1, keepdims=True).astype(jnp.int32)
    target = route * cap + slot
    taken = lax.broadcasted_iota(jnp.int32, (shard, slots), 1) == target
    taken_ref[...] = taken.astype(bf16)
    copies[1].wait()
    opened = as_column(1.0 / (1.0 + jnp.exp(-logit_ref[...])))
    lit = jnp.sum(jnp.where(taken, opened, 0.0), axis=0, keepdims=True)
    lit_ref[...] = lit
    copies[2].wait()
    width = gain_ref.shape[0]
    gain = gain_ref[...].reshape(1, width)
    none = [jnp.zeros((1, width), bf16)] * 3
    if experts == 2:
        full = [split(jnp.concatenate([part, jnp.zeros((1, width - cap), f32)], axis=1)) for part in (lit[:, :cap], lit[:, cap:])]
    else:
        full = [none]
    for ref, part, top in zip(extra_refs, full, (split(gain), none)):
        ref[...] = jnp.concatenate([*top, *part, jnp.zeros((EXTRA - 6, width), bf16)], axis=0)
    for c in copies[3:]:
        c.wait()


def attend_body(group, blocks, plane, layout, where_ref, q_ref, res_ref, taken_ref, *refs):
    kv_refs = refs[:blocks]
    extra_refs = refs[blocks : blocks + 1]
    stream_ref = refs[blocks + 1]
    send_refs = refs[blocks + 2 :]
    shard = q_ref.shape[0]
    me = where_ref[0] // plane
    rows = lax.broadcasted_iota(jnp.int32, (shard, shard), 0)
    cols = lax.broadcasted_iota(jnp.int32, (shard, shard), 1)
    nt = (((1,), (1,)), ((), ()))
    pieces = []
    for h in range(q_ref.shape[1] // HD):
        g = h // group
        q = q_ref[:, h * HD : (h + 1) * HD]
        scores = []
        for b in range(blocks):
            s = lax.dot_general(q, kv_refs[b][:shard, g * HD : (g + 1) * HD], nt, preferred_element_type=f32)
            s = s * HD ** (-0.5)
            ok = cols <= rows if b == 0 else cols < jnp.where((me ^ b) < me, shard, 0)
            scores.append(jnp.where(ok, s, floor_score))
        top = jnp.max(functools.reduce(jnp.maximum, scores), axis=1, keepdims=True)
        weights = [jnp.exp(s - top) for s in scores]
        total = jnp.sum(functools.reduce(jnp.add, weights), axis=1, keepdims=True)
        acc = jnp.zeros((shard, HD), f32)
        for b in range(blocks):
            acc += jnp.dot(weights[b].astype(bf16), kv_refs[b][shard:, g * HD : (g + 1) * HD], preferred_element_type=f32)
        pieces.append(acc / total)
    stream = (res_ref[...].astype(f32) + jnp.concatenate(pieces, axis=1)).astype(bf16)
    stream_ref[...] = stream
    tn = (((0,), (0,)), ((), ()))
    send = lax.dot_general(taken_ref[...], stream, tn, preferred_element_type=f32).astype(bf16)
    for ref, (at, rows, extra) in zip(send_refs, layout):
        ref[:rows] = send[at : at + rows]
        if extra:
            ref[rows:] = extra_refs[0][...]


def joined(refs, spans):
    parts = [refs[i][at : at + rows] for i, at, rows in spans]
    return parts[0] if len(parts) == 1 else jnp.concatenate(parts, axis=0)


def whole(ref, row, lane, width):
    return sum(ref[row + i : row + i + 1, lane : lane + width].astype(f32) for i in range(3))


def load_body(*refs):
    n = len(refs) // 2
    sems = refs[-1]
    copies = [pltpu.make_async_copy(refs[i], refs[n + i], sems.at[i]) for i in range(n)]
    for c in copies:
        c.start()
    for c in copies:
        c.wait()


def load(arrays):
    n = len(arrays)
    return kernel(
        load_body, [pltpu.VMEM(a.shape, a.dtype) for a in arrays], [RAW] * n, [VMEM] * n, 4,
        scratch=[pltpu.SemaphoreType.DMA((n,))],
    )(*[pltpu.with_memory_space_constraint(a, pltpu.HBM) for a in arrays])


def join_body(keep_ref, got_ref, extra_ref, out_ref):
    cap = got_ref.shape[0]
    out_ref[:cap] = keep_ref[:cap]
    out_ref[cap : 2 * cap] = got_ref[...]
    own, got = keep_ref[cap:], extra_ref[...]
    both = jnp.concatenate([own[3:6, :HD], got[3:6, :HD], own[3:6, 2 * HD :]], axis=1)
    out_ref[2 * cap :] = jnp.concatenate([own[:3], both, own[6:]], axis=0)


def mlp_body(ff, spec, lit_of, begun, where_ref, *refs):
    refs = list(refs)
    acc_in = [refs.pop(0) for _ in range(3)] if begun else None
    blocks = [([refs.pop(0) for _ in range(n)], spans, gain, i) for n, spans, gain, i in spec]
    lits = [refs.pop(0) for _ in lit_of]
    gates, ups = ([refs.pop(0) for _ in range(2)] for _ in range(2))
    mine = lax.rem(where_ref[0], ff)
    g, u, squares = ([None, None], [None, None], None)
    if begun:
        hidden = gates[0].shape[1]
        g = [acc_in[0][:, k * hidden : (k + 1) * hidden] for k in range(2)]
        u = [acc_in[1][:, k * hidden : (k + 1) * hidden] for k in range(2)]
        squares = acc_in[2][:, :1]

    def plus(x, y):
        return y if x is None else x + y

    for arrays, spans, gain_row, i in blocks:
        at = mine ^ i
        wide = joined(arrays, spans).astype(f32)
        quarter = wide.shape[1]
        squares = plus(squares, jnp.sum(wide * wide, axis=1, keepdims=True))
        x = (wide * whole(arrays[0], gain_row, 0, quarter)).astype(bf16)
        part = pl.ds(pl.multiple_of(at * quarter, quarter), quarter)
        for k in range(2):
            g[k] = plus(g[k], jnp.dot(x, gates[k][part, :], preferred_element_type=f32))
            u[k] = plus(u[k], jnp.dot(x, ups[k][part, :], preferred_element_type=f32))
    if not lit_of:
        g_ref, u_ref, s_ref = refs
        g_ref[...] = jnp.concatenate(g, axis=1)
        u_ref[...] = jnp.concatenate(u, axis=1)
        s_ref[...] = jnp.broadcast_to(squares, s_ref.shape)
        return
    downs = [refs.pop(0) for _ in range(2)]
    outs = refs
    rows, quarter = outs[0].shape
    opened = [as_column(whole(ref, *place)) for ref, place in zip(lits, lit_of)]
    opened = opened[0] if len(opened) == 1 else jnp.concatenate(opened, axis=0)
    factor = lax.rsqrt(squares / (4 * quarter) + norm_eps) * opened
    act = []
    for k in range(2):
        gate, up = g[k] * factor, u[k] * factor
        act.append((gate / (1.0 + jnp.exp(-gate)) * up).astype(bf16))
    for i in (3, 1, 2, 0):
        at = mine ^ i
        part = pl.ds(pl.multiple_of(at * quarter, quarter), quarter)
        y = jnp.dot(act[0], downs[0][:, part], preferred_element_type=f32)
        y += jnp.dot(act[1], downs[1][:, part], preferred_element_type=f32)
        y = y.astype(bf16)
        if i < 3 or len(outs) == 4:
            outs[i][...] = y
        else:
            outs[3][...] = y[: rows // 2]
            outs[4][...] = y[rows // 2 :]


def mlp(mine, blocks, weights, begun=None, lits=(), halve=False):
    spec = [(len(arrays), spans, gain, i) for arrays, spans, gain, i in blocks]
    rows, quarter = sum(n for _, _, n in blocks[0][1]), blocks[0][0][0].shape[1]
    flat = [*(begun or ()), *[a for arrays, *_ in blocks for a in arrays], *[a for a, *_ in lits]]
    hidden = weights[0].shape[1]
    flops = 2 * rows * quarter * len(blocks) * hidden * 4
    if lits:
        out = [pltpu.VMEM((rows, quarter), bf16)] * 3
        out += [pltpu.VMEM((rows // 2, quarter), bf16)] * 2 if halve else out[:1]
        flops += 2 * rows * quarter * 4 * hidden * 2
    else:
        out = [pltpu.VMEM((rows, 2 * hidden), f32)] * 2 + [pltpu.VMEM((rows, HD), f32)]
        weights = weights[:4]
    weights = [pltpu.with_memory_space_constraint(w, pltpu.VMEM) for w in weights]
    return kernel(
        functools.partial(mlp_body, lax.axis_size("ff"), spec, [tuple(place) for _, *place in lits], begun is not None),
        out,
        [SMEM] + [VMEM] * (len(flat) + len(weights)),
        [VMEM] * len(out),
        12,
        cost=pl.CostEstimate(flops=flops, bytes_accessed=8 << 20, transcendentals=0),
    )(mine, *flat, *weights)


def add(*parts):
    total = parts[0].astype(f32)
    for part in parts[1:]:
        total = total + part.astype(f32)
    return total.astype(bf16)


def sum_body(tops, *refs):
    out_ref = refs[-1]
    rows = out_ref.shape[0]
    total = refs[0][tops[0] : tops[0] + rows].astype(f32)
    for ref, top in zip(refs[1:-1], tops[1:]):
        total += ref[top : top + rows].astype(f32)
    out_ref[...] = total.astype(bf16)


def sum_rows(rows, *parts):
    shape = (rows, parts[0][0].shape[1])
    return kernel(
        functools.partial(sum_body, [top for _, top in parts]), pltpu.VMEM(shape, bf16), [VMEM] * len(parts), VMEM, 4
    )(*[a for a, _ in parts])


def final_body(shape, stream_ref, taken_ref, *refs):
    refs = list(refs)
    out_ref = refs.pop()
    total = stream_ref[...].astype(f32)
    at = 0
    for n in shape:
        part = refs.pop(0)[...]
        for _ in range(n - 1):
            part = (part.astype(f32) + refs.pop(0)[...].astype(f32)).astype(bf16)
        rows = part.shape[0]
        total += jnp.dot(taken_ref[:, at : at + rows], part, preferred_element_type=f32)
        at += rows
    out_ref[0] = total.astype(bf16)


def body(
    query_proj,
    key_proj,
    value_proj,
    residual,
    norm_gain,
    router_logit,
    expert_ids,
    gate_weight,
    up_weight,
    down_weight,
):
    shard, quarter = query_proj.shape[1:]
    seq, experts = lax.axis_size("seq"), lax.axis_size("exp")
    ff = lax.axis_size("ff")
    place = lax.axis_index(("seq", "exp", "ff")).astype(jnp.int32)[None]
    cap = max(2, 3 * shard // (2 * experts))
    slots = experts * cap
    two = experts == 2
    like = jax.ShapeDtypeStruct

    def far_off(x):
        return pltpu.with_memory_space_constraint(x, pltpu.HBM)

    dma = pltpu.SemaphoreType.DMA
    near = pltpu.VMEM
    kv = kernel(
        pack_body, near((2 * shard, key_proj.shape[2]), bf16), [RAW] * 2, VMEM, 4, scratch=[dma((2,))],
    )(far_off(key_proj), far_off(value_proj))
    kv2 = flip(kv, later=2, seq=2)
    kv1 = flip(kv, later=1, seq=1)
    kv3 = flip(kv2, seq=1)
    extras = 2 if two else 1
    query, res, taken, *extra, lit = kernel(
        functools.partial(prep_body, experts, ff, cap),
        (
            near((shard, quarter), bf16),
            near((shard, quarter), bf16),
            near((shard, slots), bf16),
            *[near((EXTRA, quarter), bf16)] * extras,
            near((1, slots), f32),
        ),
        [SMEM] + [RAW] * 5,
        (VMEM,) * (4 + extras),
        8,
        scratch=[near((1, shard), jnp.int32), near((1, shard), f32), near((quarter,), f32), dma((5,))],
    )(place, far_off(query_proj), far_off(residual), far_off(expert_ids[0, :, 0][None]), far_off(router_logit), far_off(norm_gain))

    layout = [(0, cap, True), (cap, cap, False)] if two else [(0, slots, False)]
    stream, *send = kernel(
        functools.partial(attend_body, HEADS // KVH, seq, experts * ff, layout),
        [near((shard, quarter), bf16)] + [near((n + (EXTRA if e else 0), quarter), bf16) for _, n, e in layout],
        [SMEM] + [VMEM] * (4 + seq),
        (VMEM,) * (1 + len(layout)),
        8,
    )(place, query, res, taken, kv, kv1, kv2, kv3, extra[0])

    rows = 2 * cap if two else slots
    if two:
        got = flip(send[1], seq=1)
        halves = [send[0], got]
        block = kernel(join_body, near((rows + EXTRA, quarter), bf16), [VMEM] * 3, VMEM, 4)(*halves, flip(extra[1], seq=1))
        lit_of = ((rows + 3, 0, cap), (rows + 3, HD, cap))
        spans, gain_row = ((0, 0, cap), (1, 0, cap)), cap
    else:
        block = lax.all_to_all(send[0], "exp", split_axis=0, concat_axis=0, tiled=True)
        lit = lax.all_to_all(lit[0], "exp", split_axis=0, concat_axis=0, tiled=True)
        lit = jnp.pad(jnp.stack(split(lit)), ((0, 0), (0, quarter - slots)))
        block = jnp.concatenate([block, extra[0][:3], lit, extra[0][6:]], axis=0)
        halves = [block]
        lit_of = ((rows + 3, 0, slots),)
        spans, gain_row = ((0, 0, rows),), rows

    def each(arrays, *args, **bits):
        return [flip(a, *args, **bits) for a in arrays]

    weights = (gate_weight[0], up_weight[0], down_weight[0])
    sel = each(halves, two, ff=2)
    non = flip(block, two, ff=1)
    own_x = flip(block, two, seq=2)
    own = flip(block, two) if two else block
    partner = each(weights, seq=1)
    pairs = [w for both in zip(load(weights), partner) for w in both]
    far = each(sel, ff=1)
    sel_x = each(sel, seq=2)
    non_x = flip(non, seq=2)
    far_x = each(sel_x, ff=1)

    def blocks(*parts):
        return [([a], ((0, 0, rows),), rows, i) if not isinstance(a, list) else (a, spans, gain_row, i) for a, i in parts]

    def lit_in(array):
        return [(array, *place) for place in lit_of]

    begun = mlp(place, blocks((own, 0), (sel, 2), (non, 1)), pairs)
    p0, p1, p2, *p3 = mlp(place, blocks((far, 3)), pairs, begun, lit_in(own), two)
    begun = mlp(place, blocks((own_x, 0), (sel_x, 2), (non_x, 1)), pairs)
    o0, o1, o2, *o3 = mlp(place, blocks((far_x, 3)), pairs, begun, lit_in(own_x), two)

    part = cap if two else slots
    order = range(len(o3))
    back_x = each(o3, ff=1)
    back = each(p3, ff=1)
    over = each([sum_rows(part, (o2, i * part), (back_x[i], 0)) for i in order], seq=2)
    last = [sum_rows(part, (p2, i * part), (back[i], 0), (over[i], 0)) for i in order]
    last = each(last, two, ff=2)
    tot_non = sum_rows(rows, (p1, 0), (flip(o1, seq=2), 0))
    home = flip(p0, two) if two else p0
    most = [home, flip(o0, two, seq=2), flip(tot_non, two, ff=1)]
    most = [sum_rows(part, *[(a, i * part) for a in most]) for i in order]
    if two:
        parts = [most[0], last[0], flip(most[1], seq=1), flip(last[1], seq=1)]
        shape = (2, 2)
    else:
        parts = [lax.all_to_all(add(most[0], last[0]), "exp", split_axis=0, concat_axis=0, tiled=True)]
        shape = (1,)
    return kernel(
        functools.partial(final_body, shape), like((1, shard, quarter), bf16), [VMEM] * (2 + len(parts)), VMEM, 8
    )(stream, taken, *parts)


def solution(mesh):
    placed = (
        P("exp", "seq", "ff"),
        P("exp", "seq", "ff"),
        P("exp", "seq", "ff"),
        P("exp", "seq", "ff"),
        P("ff"),
        P("exp", "seq"),
        P("exp", "seq", None),
        P("exp", None, ("seq", "ff")),
        P("exp", None, ("seq", "ff")),
        P("exp", ("seq", "ff"), None),
    )

    return jax.shard_map(body, mesh=mesh, in_specs=placed, out_specs=P("exp", "seq", "ff"), check_vma=False)
```
